128 devices in a mesh: grp: 4 (over x), blk: 32 (over z, y, core).
Axes of the slice: x: 4, y: 4, z: 4, core: 2. Of those that a mesh axis runs over, the one named last changes fastest.
Arguments:
- embeddings: bfloat16 [32768, 1024], P(('grp', 'blk')), may hold values from -40 to 40
- cluster_ids: int32 [32768], P(('grp', 'blk')), may hold values from 0 to 15, as said below
Outputs:
- dup_score: float32 [32768], P(('grp', 'blk'))
The draws below stay inside these ranges and needn't reach their ends.
Inputs may be any that keep to these rules, and one draw needn't show every extreme that they name: `cluster_ids`: cluster c belongs to owner group c // 4. Among the rows of one device at most 32 belong to any one cluster; in every draw there is an owner group each of whose clusters has exactly 32 rows on every device.
All inputs are finite; a program needn't handle non-finite values.
Results may differ from the reference program's by a relative error of at most 0.00041.
Values may be sent and summed in bfloat16 or wider, within the bound.
A program may use at most 64 MiB of HBM per device.

```python
import jax
import jax.numpy as jnp
from jax import lax

D = 1024
ROWS_DEV = 256
CLUS_GRP = 4
CLUSTERS = 16
CAPC = 32
DOCS = 32768
N_GRP = 4
N_BLK = 32


def joint_ids(key):
    base_key = jax.random.fold_in(key, 11)
    device_count = N_GRP * N_BLK
    slot_total = 2 * ROWS_DEV
    per_cluster = slot_total // CLUSTERS
    favour_key, order_key = jax.random.split(base_key, 2)
    favoured = jax.random.randint(favour_key, (), 0, N_GRP)
    slot_cluster = jnp.arange(slot_total, dtype=jnp.int32) // per_cluster
    slot_owner = slot_cluster // CLUS_GRP

    def one_device(device_key):
        pick_key, shuffle_key = jax.random.split(device_key)
        shuffled = jax.random.permutation(pick_key, slot_total)
        priority = shuffled + jnp.where(slot_owner == favoured, 0, slot_total)
        chosen = slot_cluster[jnp.argsort(priority)[:ROWS_DEV]]
        return jax.random.permutation(shuffle_key, chosen)
    labels = jax.vmap(one_device)(jax.random.split(order_key, device_count))
    return labels.reshape(-1).astype(jnp.int32)


def draw_cluster_ids(key, part):
    return joint_ids(key)


def draw_embeddings(key, part):
    labels = joint_ids(key)
    base_key = jax.random.fold_in(key, 23)
    sub_keys = jax.random.split(base_key, 7)
    family_count = max(DOCS // (CLUSTERS * 8), 2)
    family = jnp.minimum(jax.random.randint(sub_keys[0], (DOCS,), 0, family_count), jax.random.randint(sub_keys[1], (DOCS,), 0, family_count))
    family_row = labels * family_count + family
    family_weight = jnp.exp(jax.random.uniform(sub_keys[2], (DOCS, 1), jnp.float32, jnp.log(0.6), jnp.log(1.2)))
    noise_weight = jax.random.uniform(sub_keys[3], (DOCS, 1), jnp.float32, 0.3, 0.6)
    centers = jax.random.normal(sub_keys[4], (CLUSTERS, D), jnp.float32)
    families = jax.random.normal(sub_keys[5], (CLUSTERS * family_count, D), jnp.float32)
    noise_part = jax.random.normal(sub_keys[6], (DOCS, D), jnp.float32)
    mixture = 0.5 * centers[labels] + family_weight * families[family_row] + noise_weight * noise_part
    return jnp.clip(mixture, -40.0, 40.0).astype(jnp.bfloat16)


def setup_inputs(seed: int = 0) -> dict:
    arg_keys = jax.random.split(jax.random.key(seed), 3)
    return {
        "embeddings": draw_embeddings(jax.random.fold_in(arg_keys[2], 71), 0),
        "cluster_ids": draw_cluster_ids(jax.random.fold_in(arg_keys[2], 71), 0),
    }


def reference(embeddings, cluster_ids):
    widened = embeddings.astype(jnp.float32)
    squared = lax.optimization_barrier(jnp.sum(widened * widened, axis=1, keepdims=True)) + 1e-06
    inverse_norm = lax.rsqrt(squared)
    unit_rows = (widened * inverse_norm).astype(jnp.bfloat16)
    ordering = jnp.argsort(cluster_ids, stable=True).astype(jnp.int32)
    cluster_sizes = jnp.zeros((CLUSTERS,), jnp.int32).at[cluster_ids].add(jnp.ones((DOCS,), jnp.int32))
    starts = (jnp.cumsum(cluster_sizes) - cluster_sizes).astype(jnp.int32)
    largest = N_GRP * N_BLK * CAPC
    padded = jnp.concatenate([ordering, jnp.zeros((largest,), jnp.int32)])

    def one_cluster(cluster_index):
        picked = lax.dynamic_slice_in_dim(padded, starts[cluster_index], largest).astype(jnp.int32)
        positions = jnp.arange(largest, dtype=jnp.int32)
        alive_mask = positions < cluster_sizes[cluster_index]
        chosen_rows = unit_rows[picked]
        similar = jnp.dot(chosen_rows, chosen_rows.T, preferred_element_type=jnp.float32)
        weights = jax.nn.sigmoid(20.0 * (similar - 0.7))
        keep_mask = alive_mask[:, None] & alive_mask[None, :] & (positions[:, None] != positions[None, :])
        row_sums = lax.optimization_barrier(jnp.sum(jnp.where(keep_mask, weights, jnp.zeros_like(weights)), axis=1))
        return (jnp.where(alive_mask, row_sums, jnp.zeros_like(row_sums)), picked)
    sums_all, picked_all = lax.map(one_cluster, jnp.arange(CLUSTERS, dtype=jnp.int32))
    soft = jnp.zeros((DOCS,), jnp.float32).at[picked_all.reshape(-1)].add(sums_all.reshape(-1))
    return jnp.log1p(soft)
```

```python
import functools

import jax
import jax.numpy as jnp
from jax import lax
from jax.experimental import pallas as pl
from jax.experimental.pallas import tpu as pltpu
from jax.sharding import PartitionSpec as P

MESH = pl.DeviceIdType.MESH
ROWS = 256
FEAT = 1024
SLOT = 32
BLOCK = 16 * SLOT
PART = 4 * SLOT
ORDER = (0, 1, 3, 2)
LOG2E = 1.4426950408889634
SCALE = -20.0 * LOG2E
SHIFT = 14.0 * LOG2E
MARK = 1.5
f32 = jnp.float32
bf16 = jnp.bfloat16


def dot_t(a, b, precision=None):
    return lax.dot_general(
        a, b, (((1,), (1,)), ((), ())), preferred_element_type=f32, precision=precision
    )


def kernel(
    emb, ids, result,
    unit, out, own, v1, v2, p0, pv,
    r_own, r_p0, r_pv, c_v1, c_v2, m_own, m_p0, m_v1, m_v2, mc_p0, mc_pv,
    ret_out, ret_in, fin_out, fin_in,
    p1s, p1r, v1s, v1r, v2s, v2r, p0s, p0r, pvs, pvr, rs, rr, fs, fr,
):
    x = lax.axis_index("grp")
    b = lax.axis_index("blk")
    z = b // 8
    y = lax.rem(b // 2, 4)
    k = lax.rem(b, 2)
    s = 1 - 2 * k
    me = x * 4 + y

    def at(xx, yy, zz, kk):
        return (xx, zz * 8 + yy * 2 + kk)

    z_next = lax.rem(z + s + 4, 4)
    z_prev = lax.rem(z - s + 4, 4)
    z_far = lax.rem(z + 2, 4)
    down = at(x, y, z_prev, k)
    up = at(x, y, z_next, k)
    far = at(x, y, z_far, k)
    mate = at(x, y, z, 1 - k)
    cross = at(x, y, z_prev, 1 - k)

    def plane(dx, dy):
        return at(lax.rem(x + dx, 4), lax.rem(y + dy, 4), z, k)

    barrier = pltpu.get_barrier_semaphore()
    peers = [plane(r // 4, r % 4) for r in range(1, 16)] + [down, up, far, mate, cross]
    for peer in peers:
        pl.semaphore_signal(barrier, inc=1, device_id=peer, device_id_type=MESH)

    for c in range(4):
        rows = pl.ds(c * 64, 64)
        wide = emb[rows, :].astype(f32)
        squared = jnp.sum(wide * wide, axis=1, keepdims=True) + 1e-06
        unit[rows, :] = (wide * lax.rsqrt(squared)).astype(bf16)
    cluster = ids[...]
    hot = (cluster == lax.broadcasted_iota(jnp.int32, (16, ROWS), 0)).astype(f32)
    before = (
        lax.broadcasted_iota(jnp.int32, (ROWS, ROWS), 0)
        < lax.broadcasted_iota(jnp.int32, (ROWS, ROWS), 1)
    ).astype(f32).astype(bf16)
    ranks = jnp.dot(hot.astype(bf16), before, preferred_element_type=f32)
    rank = jnp.sum(hot * ranks, axis=0, keepdims=True).astype(jnp.int32)
    position = cluster * SLOT + rank
    first_lane = lax.broadcasted_iota(jnp.int32, (PART, 128), 1) == 0

    def exchange(i, dy):
        dx = ORDER[i]
        to_y = lax.rem(y + dy, 4)
        return pltpu.make_async_remote_copy(
            src_ref=out.at[i, to_y],
            dst_ref=own.at[pl.ds(pl.multiple_of(me * SLOT, SLOT), SLOT), :],
            send_sem=p1s.at[i * 4 + dy],
            recv_sem=p1r.at[i * 4 + dy],
            device_id=plane(dx, dy),
            device_id_type=MESH,
        )

    mine = pltpu.make_async_copy(
        out.at[0, y], own.at[pl.ds(pl.multiple_of(me * SLOT, SLOT), SLOT), :], p1r.at[0]
    )
    for i, dx in enumerate(ORDER):
        to_x = lax.rem(x + dx, 4)
        places = lax.broadcasted_iota(jnp.int32, (PART, ROWS), 0) + to_x * PART
        placed = (places == position).astype(f32)
        empty = jnp.sum(placed, axis=1, keepdims=True) < 0.5
        placed = placed.astype(bf16)
        for c in range(4):
            cols = pl.ds(c * 256, 256)
            moved = jnp.dot(placed, unit[:, cols], preferred_element_type=f32)
            if c == 0:
                head = jnp.where(first_lane & empty, MARK, moved[:, :128])
                moved = jnp.concatenate([head, moved[:, 128:]], axis=1)
            moved = moved.astype(bf16)
            for q in range(4):
                out[i, q, :, cols] = moved[q * SLOT : (q + 1) * SLOT, :]
        if i == 0:
            pl.semaphore_wait(barrier, len(peers))
            mine.start()
        for dy in range(4):
            if i or dy:
                exchange(i, dy).start()

    r_own[...] = jnp.zeros_like(r_own)
    r_p0[...] = jnp.zeros_like(r_p0)
    r_pv[...] = jnp.zeros_like(r_pv)
    c_v1[...] = jnp.zeros_like(c_v1)
    c_v2[...] = jnp.zeros_like(c_v2)

    def part(i):
        from_x = lax.rem(x - ORDER[i] + 4, 4)
        return pl.multiple_of(from_x * PART, PART)

    def pass_on(i, src, dst, send, recv, device):
        rows = pl.ds(part(i), PART)
        return pltpu.make_async_remote_copy(
            src_ref=src.at[rows, :],
            dst_ref=dst.at[rows, :],
            send_sem=send.at[i],
            recv_sem=recv.at[i],
            device_id=device,
            device_id_type=MESH,
        )

    to_v1 = [pass_on(i, own, v1, v1s, v1r, down) for i in range(4)]
    to_v2 = [pass_on(i, v1, v2, v2s, v2r, down) for i in range(4)]
    to_p0 = [pass_on(i, own, p0, p0s, p0r, mate) for i in range(4)]
    to_pv = [pass_on(i, v1, pv, pvs, pvr, mate) for i in range(4)]

    for i in range(4):
        for dy in range(4):
            if i or dy:
                exchange(i, dy).wait_recv()
            else:
                mine.wait()
        to_v1[i].start()
        to_p0[i].start()

    pick_row = (lax.broadcasted_iota(jnp.int32, (8, 128), 1) == 0).astype(f32).astype(bf16)
    pick_col = (lax.broadcasted_iota(jnp.int32, (128, 128), 0) == 0).astype(f32).astype(bf16)
    sum_row = (lax.broadcasted_iota(jnp.int32, (8, 128), 0) == 0).astype(f32)

    def lane_mask(block):
        return jnp.where(dot_t(pick_row, block[:, :128]) > 1.25, 0.0, 1.0)

    def row_mask(block):
        marks = jnp.dot(block[:, :128], pick_col, preferred_element_type=f32)
        return jnp.where(marks > 1.25, 0.0, 1.0)

    def meet(left, l0, right, r0, width, mask, racc, cacc=None, cmask=None, diagonal=False):
        lrows = pl.ds(l0, 256)
        similar = dot_t(left[lrows, :], right[pl.ds(r0, width), :])
        total = jnp.zeros((8, width), f32)
        for c in range(8):
            block = similar[c * 32 : (c + 1) * 32, :]
            w = 1.0 / (1.0 + jnp.exp2(block * SCALE + SHIFT))
            if diagonal:
                here = l0 + c * 32 + lax.broadcasted_iota(jnp.int32, (32, width), 0)
                there = r0 + lax.broadcasted_iota(jnp.int32, (32, width), 1)
                w = jnp.where(here == there, 0.0, w)
            rows = pl.ds(l0 + c * 32, 32)
            wr = w * mask
            if width == 256:
                wr = wr[:, :128] + wr[:, 128:]
            racc[rows, :] += wr
            if cacc is not None:
                cm = cmask[rows, :]
                if width == 256:
                    cm = jnp.concatenate([cm, cm], axis=1)
                wc = w * cm
                total = total + wc[0:8] + wc[8:16] + wc[16:24] + wc[24:32]
        if cacc is not None:
            cacc[:, pl.ds(r0, width)] += total

    def tile(n):
        return pl.multiple_of((n // 2) * 256, 256), pl.multiple_of(lax.rem(n, 2) * 256, 256)

    def half(h):
        other = lax.rem(h + k, 2)
        return pl.multiple_of(other * 256, 256)

    m_own[...] = lane_mask(own)

    def own_own(n, carry):
        l0, r0 = tile(n)
        meet(own, l0, own, r0, 256, m_own[0:1, pl.ds(r0, 256)], r_own, diagonal=True)
        return carry

    lax.fori_loop(0, 4, own_own, 0)

    def forward(i):
        to_v1[i].wait_recv()
        to_v2[i].start()
        to_pv[i].start()

    forward(0)
    for i in range(4):
        to_p0[i].wait_recv()
    m_p0[...] = lane_mask(p0)
    mc_p0[...] = row_mask(p0)
    forward(1)

    def own_p0(n, carry):
        l0, r0 = tile(n)
        meet(own, l0, p0, r0, 256, m_p0[0:1, pl.ds(r0, 256)], r_own)
        return carry

    lax.fori_loop(0, 4, own_p0, 0)
    forward(2)
    forward(3)
    m_v1[...] = lane_mask(v1)

    def p0_v1(n, carry):
        l0, r0 = half(n), pl.multiple_of(n * 256, 256)
        meet(p0, l0, v1, r0, 256, m_v1[0:1, pl.ds(r0, 256)], r_p0, c_v1, mc_p0)
        return carry

    lax.fori_loop(0, 2, p0_v1, 0)

    def give_back(j, device):
        return pltpu.make_async_remote_copy(
            src_ref=ret_out.at[j],
            dst_ref=ret_in.at[j],
            send_sem=rs.at[j],
            recv_sem=rr.at[j],
            device_id=device,
            device_id_type=MESH,
        )

    backs = [give_back(0, mate), give_back(1, up), give_back(2, cross), give_back(3, far)]

    def turned(racc):
        return dot_t(sum_row, racc[...], lax.Precision.HIGHEST)

    ret_out[0] = turned(r_p0)
    mc_pv[...] = row_mask(own)

    def own_v1(n, carry):
        l0, r0 = tile(n)
        meet(own, l0, v1, r0, 256, m_v1[0:1, pl.ds(r0, 256)], r_own, c_v1, mc_pv)
        return carry

    lax.fori_loop(0, 4, own_v1, 0)
    backs[0].start()
    for i in range(4):
        to_pv[i].wait_recv()
    mc_pv[...] = row_mask(pv)

    def pv_v1(n, carry):
        l0, r0 = half(n), pl.multiple_of(n * 256, 256)
        meet(pv, l0, v1, r0, 256, m_v1[0:1, pl.ds(r0, 256)], r_pv, c_v1, mc_pv)
        return carry

    lax.fori_loop(0, 2, pv_v1, 0)
    ret_out[1] = c_v1[...]

    for i in range(4):
        to_v2[i].wait_recv()
        r0 = part(i)
        mask = lane_mask(v2[pl.ds(r0, PART), :])
        if i == 0:
            backs[1].start()
        l0 = half(r0 // 256)
        meet(pv, l0, v2, r0, PART, mask[0:1, :], r_pv, c_v2, mc_pv)
        if i == 3:
            ret_out[3] = c_v2[...]
            ret_out[2] = turned(r_pv)

        def own_v2(n, carry):
            meet(own, pl.multiple_of(n * 256, 256), v2, r0, PART, mask[0:1, :], r_own)
            return carry

        lax.fori_loop(0, 2, own_v2, 0)
    backs[3].start()
    backs[2].start()
    total = turned(r_own)
    for back in backs:
        back.wait_recv()
    for j in range(4):
        total = total + ret_in[j]
    fin_out[...] = jnp.sum(total, axis=0, keepdims=True)
    fin_in[me] = fin_out[...]

    def finish(r):
        return pltpu.make_async_remote_copy(
            src_ref=fin_out,
            dst_ref=fin_in.at[me],
            send_sem=fs.at[r],
            recv_sem=fr.at[r],
            device_id=plane(r // 4, r % 4),
            device_id_type=MESH,
        )

    for r in range(1, 16):
        finish(r).start()
    wanted = (
        lax.broadcasted_iota(jnp.int32, (BLOCK, ROWS), 0) == me * SLOT + rank
    ).astype(f32)
    for r in range(1, 16):
        finish(r).wait_recv()
    sums = jnp.concatenate([fin_in[c] for c in range(16)], axis=0)
    found = jnp.dot(sums, wanted, preferred_element_type=f32, precision=lax.Precision.HIGHEST)
    result[...] = jnp.sum(found * hot, axis=0, keepdims=True)

    for i in range(4):
        for dy in range(4):
            if i or dy:
                exchange(i, dy).wait_send()
        to_v1[i].wait_send()
        to_v2[i].wait_send()
        to_p0[i].wait_send()
        to_pv[i].wait_send()
    for back in backs:
        back.wait_send()
    for r in range(1, 16):
        finish(r).wait_send()


def shards(embeddings, cluster_ids):
    dma = pltpu.SemaphoreType.DMA
    block = pltpu.VMEM((BLOCK, FEAT), bf16)
    racc = pltpu.VMEM((BLOCK, 128), f32)
    cacc = pltpu.VMEM((8, BLOCK), f32)
    soft = pl.pallas_call(
        kernel,
        out_shape=jax.ShapeDtypeStruct((1, ROWS), f32),
        in_specs=[pl.BlockSpec(memory_space=pltpu.VMEM)] * 2,
        out_specs=pl.BlockSpec(memory_space=pltpu.VMEM),
        scratch_shapes=[
            pltpu.VMEM((ROWS, FEAT), bf16),
            pltpu.VMEM((4, 4, SLOT, FEAT), bf16),
            block, block, block, block, block,
            racc, racc, racc, cacc, cacc, cacc, cacc, cacc, cacc, racc, racc,
            pltpu.VMEM((4, 8, BLOCK), f32),
            pltpu.VMEM((4, 8, BLOCK), f32),
            pltpu.VMEM((1, BLOCK), f32),
            pltpu.VMEM((16, 1, BLOCK), f32),
            dma((16,)), dma((16,)),
            dma((4,)), dma((4,)), dma((4,)), dma((4,)),
            dma((4,)), dma((4,)), dma((4,)), dma((4,)),
            dma((4,)), dma((4,)),
            dma((16,)), dma((16,)),
        ],
        compiler_params=pltpu.CompilerParams(
            collective_id=0, has_side_effects=True, vmem_limit_bytes=48 * 2**20
        ),
    )(embeddings, cluster_ids.reshape(1, ROWS))
    return jnp.log1p(soft.reshape(ROWS))


def solution(mesh):
    return jax.shard_map(
        shards,
        mesh=mesh,
        in_specs=(P(("grp", "blk"), None), P(("grp", "blk"))),
        out_specs=P(("grp", "blk")),
        check_vma=False,
    )
```

```python
import functools

import jax
import jax.numpy as jnp
from jax import lax
from jax.experimental import pallas as pl
from jax.experimental.pallas import tpu as pltpu
from jax.sharding import PartitionSpec as P

MESH = pl.DeviceIdType.MESH
ROWS = 256
FEAT = 1024
SLOT = 32
BLOCK = 16 * SLOT
PART = 4 * SLOT
ORDER = (0, 1, 3, 2)
TURNS = (
    [(0, dy) for dy in (0, 1, 3, 2)]
    + [(i, dy) for dy in (0, 1, 3, 2) for i in (1, 2)]
    + [(3, dy) for dy in (0, 1, 3, 2)]
)
LAG = 5
LOG2E = 1.4426950408889634
SCALE = -20.0 * LOG2E
SHIFT = 14.0 * LOG2E
MARK = 1.5
f32 = jnp.float32
bf16 = jnp.bfloat16


def dot_t(a, b, precision=None):
    return lax.dot_general(
        a, b, (((1,), (1,)), ((), ())), preferred_element_type=f32, precision=precision
    )


def kernel(
    emb_hbm, ids, result,
    emb, unit, out, own, v1, v2, p0, pv,
    r_own, r_p0, r_pv, c_v1, c_v2, m_own, m_p0, m_v1, m_v2, mc_p0, mc_pv,
    ret_out, ret_in, fin_out, fin_in,
    es, p1s, p1r, v1s, v1r, v2s, v2r, p0s, p0r, pvs, pvr, rs, rr, fs, fr,
):
    x = lax.axis_index("grp")
    b = lax.axis_index("blk")
    z = b // 8
    y = lax.rem(b // 2, 4)
    k = lax.rem(b, 2)
    s = 1 - 2 * k
    me = x * 4 + y

    def at(xx, yy, zz, kk):
        return (xx, zz * 8 + yy * 2 + kk)

    z_next = lax.rem(z + s + 4, 4)
    z_prev = lax.rem(z - s + 4, 4)
    z_far = lax.rem(z + 2, 4)
    down = at(x, y, z_prev, k)
    up = at(x, y, z_next, k)
    far = at(x, y, z_far, k)
    mate = at(x, y, z, 1 - k)
    cross = at(x, y, z_prev, 1 - k)

    def plane(dx, dy):
        return at(lax.rem(x + dx, 4), lax.rem(y + dy, 4), z, k)

    barrier = pltpu.get_barrier_semaphore()
    peers = [plane(r // 4, r % 4) for r in range(1, 16)] + [down, up, far, mate, cross]
    fetches = [
        pltpu.make_async_copy(
            emb_hbm.at[pl.ds(c * 64, 64), :], emb.at[pl.ds(c * 64, 64), :], es.at[c]
        )
        for c in range(4)
    ]
    for fetch in fetches:
        fetch.start()
    for peer in peers:
        pl.semaphore_signal(barrier, inc=1, device_id=peer, device_id_type=MESH)

    for c in range(4):
        rows = pl.ds(c * 64, 64)
        fetches[c].wait()
        wide = emb[rows, :].astype(f32)
        squared = jnp.sum(wide * wide, axis=1, keepdims=True) + 1e-06
        unit[rows, :] = (wide * lax.rsqrt(squared)).astype(bf16)
    cluster = ids[...]
    hot = (cluster == lax.broadcasted_iota(jnp.int32, (16, ROWS), 0)).astype(f32)
    before = (
        lax.broadcasted_iota(jnp.int32, (ROWS, ROWS), 0)
        < lax.broadcasted_iota(jnp.int32, (ROWS, ROWS), 1)
    ).astype(f32).astype(bf16)
    ranks = jnp.dot(hot.astype(bf16), before, preferred_element_type=f32)
    rank = jnp.sum(hot * ranks, axis=0, keepdims=True).astype(jnp.int32)
    position = cluster * SLOT + rank
    first_lane = lax.broadcasted_iota(jnp.int32, (PART, 128), 1) == 0

    def exchange(i, dy):
        dx = ORDER[i]
        to_y = lax.rem(y + dy, 4)
        return pltpu.make_async_remote_copy(
            src_ref=out.at[i, to_y],
            dst_ref=own.at[pl.ds(pl.multiple_of(me * SLOT, SLOT), SLOT), :],
            send_sem=p1s.at[i * 4 + dy],
            recv_sem=p1r.at[i * 4 + dy],
            device_id=plane(dx, dy),
            device_id_type=MESH,
        )

    mine = pltpu.make_async_copy(
        out.at[0, y], own.at[pl.ds(pl.multiple_of(me * SLOT, SLOT), SLOT), :], p1r.at[0]
    )
    for i, dx in enumerate(ORDER):
        to_x = lax.rem(x + dx, 4)
        places = lax.broadcasted_iota(jnp.int32, (PART, ROWS), 0) + to_x * PART
        placed = (places == position).astype(f32)
        empty = jnp.sum(placed, axis=1, keepdims=True) < 0.5
        placed = placed.astype(bf16)
        for c in range(4):
            cols = pl.ds(c * 256, 256)
            moved = jnp.dot(placed, unit[:, cols], preferred_element_type=f32)
            if c == 0:
                head = jnp.where(first_lane & empty, MARK, moved[:, :128])
                moved = jnp.concatenate([head, moved[:, 128:]], axis=1)
            moved = moved.astype(bf16)
            for q in range(4):
                out[i, q, :, cols] = moved[q * SLOT : (q + 1) * SLOT, :]
    pl.semaphore_wait(barrier, len(peers))
    mine.start()
    for i, dy in TURNS[1:]:
        exchange(i, dy).start()

    r_own[...] = jnp.zeros_like(r_own)
    r_p0[...] = jnp.zeros_like(r_p0)
    r_pv[...] = jnp.zeros_like(r_pv)
    c_v1[...] = jnp.zeros_like(c_v1)
    c_v2[...] = jnp.zeros_like(c_v2)

    def part(i):
        from_x = lax.rem(x - ORDER[i] + 4, 4)
        return pl.multiple_of(from_x * PART, PART)

    def pass_on(i, dy, src, dst, send, recv, device):
        slot = lax.rem(x - ORDER[i] + 4, 4) * 4 + lax.rem(y - dy + 4, 4)
        rows = pl.ds(pl.multiple_of(slot * SLOT, SLOT), SLOT)
        return pltpu.make_async_remote_copy(
            src_ref=src.at[rows, :],
            dst_ref=dst.at[rows, :],
            send_sem=send.at[i * 4 + dy],
            recv_sem=recv.at[i * 4 + dy],
            device_id=device,
            device_id_type=MESH,
        )

    def share(src, dst, send, recv):
        return pltpu.make_async_remote_copy(
            src_ref=src,
            dst_ref=dst,
            send_sem=send.at[0],
            recv_sem=recv.at[0],
            device_id=mate,
            device_id_type=MESH,
        )

    to_v1 = {t: pass_on(*t, own, v1, v1s, v1r, down) for t in TURNS}
    to_v2 = {t: pass_on(*t, v1, v2, v2s, v2r, down) for t in TURNS}
    to_p0 = share(own, p0, p0s, p0r)
    to_pv = share(v1, pv, pvs, pvr)

    def forward(t):
        to_v1[t].wait_recv()
        to_v2[t].start()

    for n, t in enumerate(TURNS):
        if n:
            exchange(*t).wait_recv()
        else:
            mine.wait()
        to_v1[t].start()
        if n >= LAG:
            forward(TURNS[n - LAG])
    to_p0.start()

    pick_row = (lax.broadcasted_iota(jnp.int32, (8, 128), 1) == 0).astype(f32).astype(bf16)
    pick_col = (lax.broadcasted_iota(jnp.int32, (128, 128), 0) == 0).astype(f32).astype(bf16)
    sum_row = (lax.broadcasted_iota(jnp.int32, (8, 128), 0) == 0).astype(f32)

    def lane_mask(block):
        return jnp.where(dot_t(pick_row, block[:, :128]) > 1.25, 0.0, 1.0)

    def row_mask(block):
        marks = jnp.dot(block[:, :128], pick_col, preferred_element_type=f32)
        return jnp.where(marks > 1.25, 0.0, 1.0)

    def meet(left, l0, right, r0, width, mask, racc, cacc=None, cmask=None, diagonal=False):
        lrows = pl.ds(l0, 256)
        similar = dot_t(left[lrows, :], right[pl.ds(r0, width), :])
        total = jnp.zeros((8, width), f32)
        for c in range(8):
            block = similar[c * 32 : (c + 1) * 32, :]
            w = 1.0 / (1.0 + jnp.exp2(block * SCALE + SHIFT))
            if diagonal:
                here = l0 + c * 32 + lax.broadcasted_iota(jnp.int32, (32, width), 0)
                there = r0 + lax.broadcasted_iota(jnp.int32, (32, width), 1)
                w = jnp.where(here == there, 0.0, w)
            rows = pl.ds(l0 + c * 32, 32)
            wr = w * mask
            if width == 256:
                wr = wr[:, :128] + wr[:, 128:]
            racc[rows, :] += wr
            if cacc is not None:
                cm = cmask[rows, :]
                if width == 256:
                    cm = jnp.concatenate([cm, cm], axis=1)
                wc = w * cm
                total = total + wc[0:8] + wc[8:16] + wc[16:24] + wc[24:32]
        if cacc is not None:
            cacc[:, pl.ds(r0, width)] += total

    def tile(n):
        return pl.multiple_of((n // 2) * 256, 256), pl.multiple_of(lax.rem(n, 2) * 256, 256)

    def half(h):
        other = lax.rem(h + k, 2)
        return pl.multiple_of(other * 256, 256)

    m_own[...] = lane_mask(own)

    for n in range(4):
        l0, r0 = tile(n)
        meet(own, l0, own, r0, 256, m_own[0:1, pl.ds(r0, 256)], r_own, diagonal=True)
        for t in TURNS[16 - LAG + 2 * n : 18 - LAG + 2 * n]:
            forward(t)
    for t in TURNS[24 - LAG :]:
        forward(t)
    to_pv.start()
    to_p0.wait_recv()
    m_p0[...] = lane_mask(p0)
    mc_p0[...] = row_mask(p0)

    def own_p0(n, carry):
        l0, r0 = tile(n)
        meet(own, l0, p0, r0, 256, m_p0[0:1, pl.ds(r0, 256)], r_own)
        return carry

    lax.fori_loop(0, 4, own_p0, 0)
    m_v1[...] = lane_mask(v1)

    def p0_v1(n, carry):
        l0, r0 = half(n), pl.multiple_of(n * 256, 256)
        meet(p0, l0, v1, r0, 256, m_v1[0:1, pl.ds(r0, 256)], r_p0, c_v1, mc_p0)
        return carry

    lax.fori_loop(0, 2, p0_v1, 0)

    def give_back(j, device):
        return pltpu.make_async_remote_copy(
            src_ref=ret_out.at[j],
            dst_ref=ret_in.at[j],
            send_sem=rs.at[j],
            recv_sem=rr.at[j],
            device_id=device,
            device_id_type=MESH,
        )

    backs = [give_back(0, mate), give_back(1, up), give_back(2, cross), give_back(3, far)]

    def turned(racc):
        return dot_t(sum_row, racc[...], lax.Precision.HIGHEST)

    ret_out[0] = turned(r_p0)
    mc_pv[...] = row_mask(own)

    def own_v1(n, carry):
        l0, r0 = tile(n)
        meet(own, l0, v1, r0, 256, m_v1[0:1, pl.ds(r0, 256)], r_own, c_v1, mc_pv)
        return carry

    lax.fori_loop(0, 4, own_v1, 0)
    backs[0].start()
    to_pv.wait_recv()
    mc_pv[...] = row_mask(pv)

    def pv_v1(n, carry):
        l0, r0 = half(n), pl.multiple_of(n * 256, 256)
        meet(pv, l0, v1, r0, 256, m_v1[0:1, pl.ds(r0, 256)], r_pv, c_v1, mc_pv)
        return carry

    lax.fori_loop(0, 2, pv_v1, 0)
    ret_out[1] = c_v1[...]

    for i in range(4):
        for dy in range(4):
            to_v2[i, dy].wait_recv()
        r0 = part(i)
        mask = lane_mask(v2[pl.ds(r0, PART), :])
        if i == 0:
            backs[1].start()
        l0 = half(r0 // 256)
        meet(pv, l0, v2, r0, PART, mask[0:1, :], r_pv, c_v2, mc_pv)
        if i == 3:
            ret_out[3] = c_v2[...]
            ret_out[2] = turned(r_pv)

        def own_v2(n, carry):
            meet(own, pl.multiple_of(n * 256, 256), v2, r0, PART, mask[0:1, :], r_own)
            return carry

        lax.fori_loop(0, 2, own_v2, 0)
    backs[3].start()
    backs[2].start()
    total = turned(r_own)
    for back in backs:
        back.wait_recv()
    for j in range(4):
        total = total + ret_in[j]
    total = jnp.sum(total, axis=0, keepdims=True)
    for j in range(4):
        fin_out[j] = total[:, j * PART : (j + 1) * PART]
    fin_in[me] = fin_out[x]

    def finish(r):
        return pltpu.make_async_remote_copy(
            src_ref=fin_out.at[lax.rem(x + r // 4, 4)],
            dst_ref=fin_in.at[me],
            send_sem=fs.at[r],
            recv_sem=fr.at[r],
            device_id=plane(r // 4, r % 4),
            device_id_type=MESH,
        )

    for r in range(1, 16):
        finish(r).start()
    wanted = (
        lax.broadcasted_iota(jnp.int32, (PART, ROWS), 0) == y * SLOT + rank
    ).astype(f32)
    for r in range(1, 16):
        finish(r).wait_recv()
    sums = jnp.concatenate([fin_in[c] for c in range(16)], axis=0)
    found = jnp.dot(sums, wanted, preferred_element_type=f32, precision=lax.Precision.HIGHEST)
    result[...] = jnp.sum(found * hot, axis=0, keepdims=True)

    for n, t in enumerate(TURNS):
        if n:
            exchange(*t).wait_send()
        to_v1[t].wait_send()
        to_v2[t].wait_send()
    to_p0.wait_send()
    to_pv.wait_send()
    for back in backs:
        back.wait_send()
    for r in range(1, 16):
        finish(r).wait_send()


def shards(embeddings, cluster_ids):
    dma = pltpu.SemaphoreType.DMA
    block = pltpu.VMEM((BLOCK, FEAT), bf16)
    racc = pltpu.VMEM((BLOCK, 128), f32)
    cacc = pltpu.VMEM((8, BLOCK), f32)
    soft = pl.pallas_call(
        kernel,
        out_shape=jax.ShapeDtypeStruct((1, ROWS), f32),
        in_specs=[
            pl.BlockSpec(memory_space=pltpu.HBM),
            pl.BlockSpec(memory_space=pltpu.VMEM),
        ],
        out_specs=pl.BlockSpec(memory_space=pltpu.VMEM),
        scratch_shapes=[
            pltpu.VMEM((ROWS, FEAT), bf16),
            pltpu.VMEM((ROWS, FEAT), bf16),
            pltpu.VMEM((4, 4, SLOT, FEAT), bf16),
            block, block, block, block, block,
            racc, racc, racc, cacc, cacc, cacc, cacc, cacc, cacc, racc, racc,
            pltpu.VMEM((4, 8, BLOCK), f32),
            pltpu.VMEM((4, 8, BLOCK), f32),
            pltpu.VMEM((4, 1, PART), f32),
            pltpu.VMEM((16, 1, PART), f32),
            dma((4,)),
            dma((16,)), dma((16,)),
            dma((16,)), dma((16,)), dma((16,)), dma((16,)),
            dma((1,)), dma((1,)), dma((1,)), dma((1,)),
            dma((4,)), dma((4,)),
            dma((16,)), dma((16,)),
        ],
        compiler_params=pltpu.CompilerParams(
            collective_id=0, has_side_effects=True, vmem_limit_bytes=48 * 2**20
        ),
    )(embeddings, cluster_ids.reshape(1, ROWS))
    return jnp.log1p(soft.reshape(ROWS))


def solution(mesh):
    return jax.shard_map(
        shards,
        mesh=mesh,
        in_specs=(P(("grp", "blk"), None), P(("grp", "blk"))),
        out_specs=P(("grp", "blk")),
        check_vma=False,
    )
```

```python
import functools

import jax
import jax.numpy as jnp
from jax import lax
from jax.experimental import pallas as pl
from jax.experimental.pallas import tpu as pltpu
from jax.sharding import PartitionSpec as P

MESH = pl.DeviceIdType.MESH
ROWS = 256
FEAT = 1024
SLOT = 32
BLOCK = 16 * SLOT
PART = 4 * SLOT
TURNS = (
    (0, 0), (0, 1), (0, 3), (0, 2),
    (1, 0), (3, 0), (1, 1), (3, 1),
    (1, 3), (3, 3), (1, 2), (3, 2),
    (2, 0), (2, 1), (2, 3), (2, 2),
)
AHEAD = 4
LAG = 4
LOG2E = 1.4426950408889634
SCALE = -20.0 * LOG2E
SHIFT = 14.0 * LOG2E
MARK = 1.5
f32 = jnp.float32
bf16 = jnp.bfloat16


def dot_t(a, b, precision=None):
    return lax.dot_general(
        a, b, (((1,), (1,)), ((), ())), preferred_element_type=f32, precision=precision
    )


def kernel(
    emb_hbm, ids, result,
    emb, unit, out, own, v1, v2, p0, pv,
    r_own, r_p0, r_pv, c_v1, c_v2, m_own, m_p0, m_v1, mc_own, mc_p0, mc_pv,
    ret_out, ret_in, fin_out, fin_in,
    es, p1s, p1r, v1s, v1r, v2s, v2r, p0s, p0r, pvs, pvr, rs, rr, fs, fr,
):
    x = lax.axis_index("grp")
    b = lax.axis_index("blk")
    z = b // 8
    y = lax.rem(b // 2, 4)
    k = lax.rem(b, 2)
    s = 1 - 2 * k

    def at(xx, yy, zz, kk):
        return (xx, zz * 8 + yy * 2 + kk)

    z_next = lax.rem(z + s + 4, 4)
    z_prev = lax.rem(z - s + 4, 4)
    z_far = lax.rem(z + 2, 4)
    down = at(x, y, z_prev, k)
    up = at(x, y, z_next, k)
    far = at(x, y, z_far, k)
    mate = at(x, y, z, 1 - k)
    cross = at(x, y, z_prev, 1 - k)

    def plane(dx, dy):
        return at(lax.rem(x + dx, 4), lax.rem(y + dy, 4), z, k)

    def piece(r, count=1):
        return pl.ds(r * SLOT, count * SLOT)

    barrier = pltpu.get_barrier_semaphore()
    peers = [plane(r // 4, r % 4) for r in range(1, 16)] + [down, up, far, mate, cross]
    fetches = [
        pltpu.make_async_copy(
            emb_hbm.at[pl.ds(c * 64, 64), :], emb.at[pl.ds(c * 64, 64), :], es.at[c]
        )
        for c in range(4)
    ]
    for fetch in fetches:
        fetch.start()
    for peer in peers:
        pl.semaphore_signal(barrier, inc=1, device_id=peer, device_id_type=MESH)

    for c in range(4):
        rows = pl.ds(c * 64, 64)
        fetches[c].wait()
        wide = emb[rows, :].astype(f32)
        squared = jnp.sum(wide * wide, axis=1, keepdims=True) + 1e-06
        unit[rows, :] = (wide * lax.rsqrt(squared)).astype(bf16)
    cluster = ids[...]
    hot = (cluster == lax.broadcasted_iota(jnp.int32, (16, ROWS), 0)).astype(f32)
    before = (
        lax.broadcasted_iota(jnp.int32, (ROWS, ROWS), 0)
        < lax.broadcasted_iota(jnp.int32, (ROWS, ROWS), 1)
    ).astype(f32).astype(bf16)
    ranks = jnp.dot(hot.astype(bf16), before, preferred_element_type=f32)
    rank = jnp.sum(hot * ranks, axis=0, keepdims=True).astype(jnp.int32)
    position = cluster * SLOT + rank
    first_lane = lax.broadcasted_iota(jnp.int32, (PART, 128), 1) == 0

    def exchange(r):
        return pltpu.make_async_remote_copy(
            src_ref=out.at[piece(r), :],
            dst_ref=own.at[piece(r), :],
            send_sem=p1s.at[r],
            recv_sem=p1r.at[r],
            device_id=plane(*TURNS[r]),
            device_id_type=MESH,
        )

    def cluster_of(r):
        dx, dy = TURNS[r]
        return lax.rem(x + dx, 4) * 4 + lax.rem(y + dy, 4)

    slots = lax.broadcasted_iota(jnp.int32, (SLOT, ROWS), 0)
    for g in range(4):
        placed = jnp.concatenate(
            [
                (slots + cluster_of(r) * SLOT == position).astype(f32)
                for r in range(4 * g, 4 * g + 4)
            ],
            axis=0,
        )
        empty = jnp.sum(placed, axis=1, keepdims=True) < 0.5
        placed = placed.astype(bf16)
        for c in range(4):
            cols = pl.ds(c * 256, 256)
            moved = jnp.dot(placed, unit[:, cols], preferred_element_type=f32)
            if c == 0:
                head = jnp.where(first_lane & empty, MARK, moved[:, :128])
                moved = jnp.concatenate([head, moved[:, 128:]], axis=1)
            moved = moved.astype(bf16)
            if g == 0:
                own[piece(0), cols] = moved[:SLOT, :]
            out[piece(4 * g, 4), cols] = moved

    pl.semaphore_wait(barrier, len(peers))
    for r in range(1, 1 + AHEAD):
        exchange(r).start()

    r_own[...] = jnp.zeros_like(r_own)
    r_p0[...] = jnp.zeros_like(r_p0)
    r_pv[...] = jnp.zeros_like(r_pv)
    c_v1[...] = jnp.zeros_like(c_v1)
    c_v2[...] = jnp.zeros_like(c_v2)

    def pass_on(r, src, dst, send, recv, device):
        return pltpu.make_async_remote_copy(
            src_ref=src.at[piece(r), :],
            dst_ref=dst.at[piece(r), :],
            send_sem=send.at[r],
            recv_sem=recv.at[r],
            device_id=device,
            device_id_type=MESH,
        )

    def share(h, src, dst, send, recv):
        rows = pl.ds(h * 256, 256)
        return pltpu.make_async_remote_copy(
            src_ref=src.at[rows, :],
            dst_ref=dst.at[rows, :],
            send_sem=send.at[h],
            recv_sem=recv.at[h],
            device_id=mate,
            device_id_type=MESH,
        )

    to_v1 = [pass_on(r, own, v1, v1s, v1r, down) for r in range(16)]
    to_v2 = [pass_on(r, v1, v2, v2s, v2r, down) for r in range(16)]
    to_p0 = [share(h, own, p0, p0s, p0r) for h in range(2)]
    to_pv = [share(h, v1, pv, pvs, pvr) for h in range(2)]

    pick_row = (lax.broadcasted_iota(jnp.int32, (8, 128), 1) == 0).astype(f32).astype(bf16)
    pick_col = (lax.broadcasted_iota(jnp.int32, (128, 128), 0) == 0).astype(f32).astype(bf16)
    sum_row = (lax.broadcasted_iota(jnp.int32, (8, 128), 0) == 0).astype(f32)

    def lane_mask(block):
        return jnp.where(dot_t(pick_row, block[:, :128]) > 1.25, 0.0, 1.0)

    def row_mask(block):
        marks = jnp.dot(block[:, :128], pick_col, preferred_element_type=f32)
        return jnp.where(marks > 1.25, 0.0, 1.0)

    def meet(left, l0, right, r0, width, mask, racc, cacc=None, cmask=None, diagonal=False):
        lrows = pl.ds(l0, 256)
        similar = dot_t(left[lrows, :], right[pl.ds(r0, width), :])
        total = jnp.zeros((8, width), f32)
        for c in range(8):
            block = similar[c * 32 : (c + 1) * 32, :]
            w = 1.0 / (1.0 + jnp.exp2(block * SCALE + SHIFT))
            if diagonal:
                here = l0 + c * 32 + lax.broadcasted_iota(jnp.int32, (32, width), 0)
                there = r0 + lax.broadcasted_iota(jnp.int32, (32, width), 1)
                w = jnp.where(here == there, 0.0, w)
            rows = pl.ds(l0 + c * 32, 32)
            wr = w * mask
            if width == 256:
                wr = wr[:, :128] + wr[:, 128:]
            racc[rows, :] += wr
            if cacc is not None:
                cm = cmask[rows, :]
                if width == 256:
                    cm = jnp.concatenate([cm, cm], axis=1)
                wc = w * cm
                total = total + wc[0:8] + wc[8:16] + wc[16:24] + wc[24:32]
        if cacc is not None:
            cacc[:, pl.ds(r0, width)] += total

    def half(h):
        return pl.multiple_of(lax.rem(h + k, 2) * 256, 256)

    def fill_lane(mask, block, h):
        rows = pl.ds(h * 256, 256)
        mask[:, rows] = lane_mask(block[rows, :128])

    def fill_row(mask, block, h):
        rows = pl.ds(h * 256, 256)
        mask[rows, :] = row_mask(block[rows, :128])

    def own_with(l, right, mask, h, cacc=None, diagonal=False):
        meet(
            own, l * 256, right, h * 256, 256, mask[0:1, pl.ds(h * 256, 256)], r_own,
            cacc, mc_own, diagonal,
        )

    def own_v1(l, h):
        own_with(l, v1, m_v1, h, c_v1)

    def forward(r):
        to_v1[r].wait_recv()
        to_v2[r].start()
        if r % 8 == 7:
            to_pv[r // 8].start()

    for n in range(16):
        if n:
            exchange(n).wait_recv()
        if n + AHEAD + 1 < 16:
            exchange(n + AHEAD + 1).start()
        to_v1[n].start()
        if n >= LAG:
            forward(n - LAG)
        if n % 8 == 7:
            to_p0[n // 8].start()
        if n == 8:
            fill_lane(m_own, own, 0)
            fill_row(mc_own, own, 0)
            own_with(0, own, m_own, 0, diagonal=True)
        if n == 10:
            to_p0[0].wait_recv()
            fill_lane(m_p0, p0, 0)
            fill_row(mc_p0, p0, 0)
            own_with(0, p0, m_p0, 0)
        if n == 12:
            fill_lane(m_v1, v1, 0)
            own_v1(0, 0)
    fill_lane(m_own, own, 1)
    own_with(0, own, m_own, 1)
    forward(12)
    own_with(1, own, m_own, 0)
    forward(13)
    own_with(1, own, m_own, 1, diagonal=True)
    forward(14)
    fill_row(mc_own, own, 1)
    own_v1(1, 0)
    forward(15)
    to_p0[1].wait_recv()
    fill_lane(m_p0, p0, 1)
    fill_row(mc_p0, p0, 1)
    own_with(0, p0, m_p0, 1)
    own_with(1, p0, m_p0, 0)
    own_with(1, p0, m_p0, 1)
    fill_lane(m_v1, v1, 1)
    own_v1(0, 1)
    own_v1(1, 1)

    def p0_v1(n, carry):
        l0, r0 = half(n), pl.multiple_of(n * 256, 256)
        meet(p0, l0, v1, r0, 256, m_v1[0:1, pl.ds(r0, 256)], r_p0, c_v1, mc_p0)
        return carry

    lax.fori_loop(0, 2, p0_v1, 0)

    def give_back(j, device):
        return pltpu.make_async_remote_copy(
            src_ref=ret_out.at[j],
            dst_ref=ret_in.at[j],
            send_sem=rs.at[j],
            recv_sem=rr.at[j],
            device_id=device,
            device_id_type=MESH,
        )

    backs = [give_back(0, mate), give_back(1, up), give_back(2, cross), give_back(3, far)]

    def turned(racc):
        return dot_t(sum_row, racc[...], lax.Precision.HIGHEST)

    ret_out[0] = turned(r_p0)
    for h in range(2):
        to_pv[h].wait_recv()
        fill_row(mc_pv, pv, h)
    backs[0].start()

    def pv_v1(n, carry):
        l0, r0 = half(n), pl.multiple_of(n * 256, 256)
        meet(pv, l0, v1, r0, 256, m_v1[0:1, pl.ds(r0, 256)], r_pv, c_v1, mc_pv)
        return carry

    lax.fori_loop(0, 2, pv_v1, 0)
    ret_out[1] = c_v1[...]

    for g in range(4):
        for r in range(4 * g, 4 * g + 4):
            to_v2[r].wait_recv()
        r0 = g * PART
        mask = lane_mask(v2[pl.ds(r0, PART), :128])
        if g == 0:
            backs[1].start()
        meet(pv, half(g // 2), v2, r0, PART, mask[0:1, :], r_pv, c_v2, mc_pv)
        if g == 3:
            ret_out[3] = c_v2[...]
            ret_out[2] = turned(r_pv)
            backs[3].start()

        def own_v2(n, carry):
            meet(own, pl.multiple_of(n * 256, 256), v2, r0, PART, mask[0:1, :], r_own)
            return carry

        lax.fori_loop(0, 2, own_v2, 0)
    backs[2].start()
    total = turned(r_own)
    for back in backs:
        back.wait_recv()
    for j in range(4):
        total = total + ret_in[j]
    total = jnp.sum(total, axis=0, keepdims=True)
    for j in range(4):
        fin_out[j] = total[:, j * PART : (j + 1) * PART]
    fin_in[0] = fin_out[0]

    def finish(r):
        dx, dy = TURNS[r]
        return pltpu.make_async_remote_copy(
            src_ref=fin_out.at[r // 4],
            dst_ref=fin_in.at[r],
            send_sem=fs.at[r],
            recv_sem=fr.at[r],
            device_id=plane(4 - dx, 4 - dy),
            device_id_type=MESH,
        )

    for r in range(15, 0, -1):
        finish(r).start()
    wanted = (slots == rank).astype(f32)
    chosen = jnp.concatenate(
        [(cluster == cluster_of(r)).astype(f32) for r in range(16)], axis=0
    )
    for r in range(1, 16):
        finish(r).wait_recv()
    sums = jnp.concatenate(
        [fin_in[r][:, (r % 4) * SLOT : (r % 4 + 1) * SLOT] for r in range(16)], axis=0
    )
    found = jnp.dot(sums, wanted, preferred_element_type=f32, precision=lax.Precision.HIGHEST)
    result[...] = jnp.sum(found * chosen, axis=0, keepdims=True)

    for r in range(16):
        if r:
            exchange(r).wait_send()
            finish(r).wait_send()
        to_v1[r].wait_send()
        to_v2[r].wait_send()
    for h in range(2):
        to_p0[h].wait_send()
        to_pv[h].wait_send()
    for back in backs:
        back.wait_send()


def shards(embeddings, cluster_ids):
    dma = pltpu.SemaphoreType.DMA
    block = pltpu.VMEM((BLOCK, FEAT), bf16)
    racc = pltpu.VMEM((BLOCK, 128), f32)
    cacc = pltpu.VMEM((8, BLOCK), f32)
    soft = pl.pallas_call(
        kernel,
        out_shape=jax.ShapeDtypeStruct((1, ROWS), f32),
        in_specs=[
            pl.BlockSpec(memory_space=pltpu.HBM),
            pl.BlockSpec(memory_space=pltpu.VMEM),
        ],
        out_specs=pl.BlockSpec(memory_space=pltpu.VMEM),
        scratch_shapes=[
            pltpu.VMEM((ROWS, FEAT), bf16),
            pltpu.VMEM((ROWS, FEAT), bf16),
            block, block, block, block, block, block,
            racc, racc, racc, cacc, cacc, cacc, cacc, cacc, racc, racc, racc,
            pltpu.VMEM((4, 8, BLOCK), f32),
            pltpu.VMEM((4, 8, BLOCK), f32),
            pltpu.VMEM((4, 1, PART), f32),
            pltpu.VMEM((16, 1, PART), f32),
            dma((4,)),
            dma((16,)), dma((16,)),
            dma((16,)), dma((16,)), dma((16,)), dma((16,)),
            dma((2,)), dma((2,)), dma((2,)), dma((2,)),
            dma((4,)), dma((4,)),
            dma((16,)), dma((16,)),
        ],
        compiler_params=pltpu.CompilerParams(
            collective_id=0, has_side_effects=True, vmem_limit_bytes=48 * 2**20
        ),
    )(embeddings, cluster_ids.reshape(1, ROWS))
    return jnp.log1p(soft.reshape(ROWS))


def solution(mesh):
    return jax.shard_map(
        shards,
        mesh=mesh,
        in_specs=(P(("grp", "blk"), None), P(("grp", "blk"))),
        out_specs=P(("grp", "blk")),
        check_vma=False,
    )
```

```python
import functools

import jax
import jax.numpy as jnp
from jax import lax
from jax.experimental import pallas as pl
from jax.experimental.pallas import tpu as pltpu
from jax.sharding import PartitionSpec as P

MESH = pl.DeviceIdType.MESH
ROWS = 256
FEAT = 1024
SLOT = 32
BLOCK = 16 * SLOT
PART = 4 * SLOT
TURNS = (
    (0, 0), (0, 1), (1, 0), (0, 3), (3, 0), (1, 1), (3, 3), (1, 3),
    (3, 1), (0, 2), (2, 0), (2, 1), (1, 2), (2, 3), (3, 2), (2, 2),
)
AHEAD = 4
LOG2E = 1.4426950408889634
SCALE = -20.0 * LOG2E
SHIFT = 14.0 * LOG2E
MARK = 1.5
f32 = jnp.float32
bf16 = jnp.bfloat16


def dot_t(a, b, precision=None):
    return lax.dot_general(
        a, b, (((1,), (1,)), ((), ())), preferred_element_type=f32, precision=precision
    )


def kernel(
    emb_hbm, ids, result,
    emb, unit, out, own, near, back, p0,
    r_own, r_back, c_near, m_own, m_p0, m_near, mc_own, mc_back,
    ret_out, ret_in, fin_out, fin_in,
    es, p1s, p1r, ns, nr, bs, br, p0s, p0r, xs, xr, rs, rr, fs, fr,
):
    x = lax.axis_index("grp")
    b = lax.axis_index("blk")
    z = b // 8
    y = lax.rem(b // 2, 4)
    k = lax.rem(b, 2)

    def at(xx, yy, zz, kk):
        return (xx, zz * 8 + yy * 2 + kk)

    z_up = lax.rem(z + 1, 4)
    z_down = lax.rem(z + 3, 4)
    up = at(x, y, z_up, k)
    down = at(x, y, z_down, k)
    up_mate = at(x, y, z_up, 1 - k)
    down_mate = at(x, y, z_down, 1 - k)
    mate = at(x, y, z, 1 - k)
    pick = z // 2

    def plane(dx, dy):
        return at(lax.rem(x + dx, 4), lax.rem(y + dy, 4), z, k)

    def piece(r, count=1):
        return pl.ds(r * SLOT, count * SLOT)

    barrier = pltpu.get_barrier_semaphore()
    peers = [plane(r // 4, r % 4) for r in range(1, 16)] + [
        up, down, mate, up_mate, down_mate
    ]
    fetches = [
        pltpu.make_async_copy(
            emb_hbm.at[pl.ds(c * 64, 64), :], emb.at[pl.ds(c * 64, 64), :], es.at[c]
        )
        for c in range(4)
    ]
    for fetch in fetches:
        fetch.start()
    for peer in peers:
        pl.semaphore_signal(barrier, inc=1, device_id=peer, device_id_type=MESH)

    for c in range(4):
        rows = pl.ds(c * 64, 64)
        fetches[c].wait()
        wide = emb[rows, :].astype(f32)
        squared = jnp.sum(wide * wide, axis=1, keepdims=True) + 1e-06
        unit[rows, :] = (wide * lax.rsqrt(squared)).astype(bf16)
    cluster = ids[...]
    hot = (cluster == lax.broadcasted_iota(jnp.int32, (16, ROWS), 0)).astype(f32)
    before = (
        lax.broadcasted_iota(jnp.int32, (ROWS, ROWS), 0)
        < lax.broadcasted_iota(jnp.int32, (ROWS, ROWS), 1)
    ).astype(f32).astype(bf16)
    ranks = jnp.dot(hot.astype(bf16), before, preferred_element_type=f32)
    rank = jnp.sum(hot * ranks, axis=0, keepdims=True).astype(jnp.int32)
    position = cluster * SLOT + rank
    first_lane = lax.broadcasted_iota(jnp.int32, (PART, 128), 1) == 0

    def exchange(r):
        return pltpu.make_async_remote_copy(
            src_ref=out.at[piece(r), :],
            dst_ref=own.at[piece(r), :],
            send_sem=p1s.at[r],
            recv_sem=p1r.at[r],
            device_id=plane(*TURNS[r]),
            device_id_type=MESH,
        )

    def cluster_of(r):
        dx, dy = TURNS[r]
        return lax.rem(x + dx, 4) * 4 + lax.rem(y + dy, 4)

    slots = lax.broadcasted_iota(jnp.int32, (SLOT, ROWS), 0)
    for g in range(4):
        placed = jnp.concatenate(
            [
                (slots + cluster_of(r) * SLOT == position).astype(f32)
                for r in range(4 * g, 4 * g + 4)
            ],
            axis=0,
        )
        empty = jnp.sum(placed, axis=1, keepdims=True) < 0.5
        placed = placed.astype(bf16)
        for c in range(4):
            cols = pl.ds(c * 256, 256)
            moved = jnp.dot(placed, unit[:, cols], preferred_element_type=f32)
            if c == 0:
                head = jnp.where(first_lane & empty, MARK, moved[:, :128])
                moved = jnp.concatenate([head, moved[:, 128:]], axis=1)
            moved = moved.astype(bf16)
            if g == 0:
                own[piece(0), cols] = moved[:SLOT, :]
            out[piece(4 * g, 4), cols] = moved

    pl.semaphore_wait(barrier, len(peers))
    for r in range(1, 1 + AHEAD):
        exchange(r).start()

    for sums in (r_own, r_back, c_near):
        sums[...] = jnp.zeros_like(sums)

    def pass_on(r, src, dst, send, recv, device):
        return pltpu.make_async_remote_copy(
            src_ref=src.at[piece(r), :],
            dst_ref=dst.at[piece(r), :],
            send_sem=send.at[r],
            recv_sem=recv.at[r],
            device_id=device,
            device_id_type=MESH,
        )

    def share(n, size, src, dst, send, recv):
        rows = pl.ds(n * size, size)
        return pltpu.make_async_remote_copy(
            src_ref=src.at[rows, :],
            dst_ref=dst.at[rows, :],
            send_sem=send.at[n],
            recv_sem=recv.at[n],
            device_id=mate,
            device_id_type=MESH,
        )

    to_near = [pass_on(r, own, near.at[0], ns, nr, down) for r in range(16)]
    to_back = [pass_on(r, own, back, bs, br, up) for r in range(16)]
    to_p0 = [share(h, 256, own, p0, p0s, p0r) for h in range(2)]
    to_mate = [share(g, PART, near.at[0], near.at[1], xs, xr) for g in range(4)]

    pick_row = (lax.broadcasted_iota(jnp.int32, (8, 128), 1) == 0).astype(f32).astype(bf16)
    pick_col = (lax.broadcasted_iota(jnp.int32, (128, 128), 0) == 0).astype(f32).astype(bf16)
    sum_row = (lax.broadcasted_iota(jnp.int32, (8, 128), 0) == 0).astype(f32)

    def lane_mask(block):
        return jnp.where(dot_t(pick_row, block[:, :128]) > 1.25, 0.0, 1.0)

    def row_mask(block):
        marks = jnp.dot(block[:, :128], pick_col, preferred_element_type=f32)
        return jnp.where(marks > 1.25, 0.0, 1.0)

    def meet(
        left, l0, height, right, r0, width, mask, racc,
        cacc=None, cmask=None, diagonal=False,
    ):
        similar = dot_t(left[pl.ds(l0, height), :], right[pl.ds(r0, width), :])
        total = jnp.zeros((8, width), f32)
        for c in range(height // 32):
            block = similar[c * 32 : (c + 1) * 32, :]
            w = 1.0 / (1.0 + jnp.exp2(block * SCALE + SHIFT))
            if diagonal:
                here = l0 + c * 32 + lax.broadcasted_iota(jnp.int32, (32, width), 0)
                there = r0 + lax.broadcasted_iota(jnp.int32, (32, width), 1)
                w = jnp.where(here == there, 0.0, w)
            rows = pl.ds(l0 + c * 32, 32)
            wr = w * mask[0:1, pl.ds(r0, width)]
            if width == 256:
                wr = wr[:, :128] + wr[:, 128:]
            racc[rows, :] += wr
            if cacc is not None:
                cm = cmask[rows, :]
                if width == 256:
                    cm = jnp.concatenate([cm, cm], axis=1)
                wc = w * cm
                total = total + wc[0:8] + wc[8:16] + wc[16:24] + wc[24:32]
        if cacc is not None:
            cacc[:, pl.ds(r0, width)] += total

    def fill_lane(mask, block, r0, size):
        rows = pl.ds(r0, size)
        mask[:, rows] = lane_mask(block[rows, :128])

    def fill_row(mask, block, r0, size):
        rows = pl.ds(r0, size)
        mask[rows, :] = row_mask(block[rows, :128])

    def own_own(l, h):
        meet(own, l * 256, 256, own, h * 256, 256, m_own, r_own, diagonal=l == h)

    def own_p0(l, h):
        meet(own, l * 256, 256, p0, h * 256, 256, m_p0, r_own)

    def own_near(j, r0, width):
        def body(l, carry):
            l0 = pl.multiple_of(l * 256, 256)
            meet(
                own, l0, 256, near.at[j], r0, width, m_near.at[j], r_own,
                c_near.at[j], mc_own,
            )
            return carry

        lax.fori_loop(0, 2, body, 0)

    def back_near(l0, height, r0, width):
        meet(
            back, l0, height, near.at[pick], r0, width, m_near.at[pick], r_back,
            c_near.at[pick], mc_back,
        )

    def landed(g):
        for r in range(4 * g, 4 * g + 4):
            to_near[r].wait_recv()
        to_mate[g].start()
        fill_lane(m_near.at[0], near.at[0], g * PART, PART)

    def behind(g):
        for r in range(4 * g, 4 * g + 4):
            to_back[r].wait_recv()
        fill_row(mc_back, back, g * PART, PART)

    def mated(g):
        to_mate[g].wait_recv()
        fill_lane(m_near.at[1], near.at[1], g * PART, PART)

    for n in range(16):
        if n:
            exchange(n).wait_recv()
        if n + AHEAD + 1 < 16:
            exchange(n + AHEAD + 1).start()
        to_near[n].start()
        to_back[n].start()
        if n % 8 == 7:
            to_p0[n // 8].start()
        if n == 8:
            fill_lane(m_own, own, 0, 256)
            fill_row(mc_own, own, 0, 256)
        if n == 9:
            own_own(0, 0)
        if n == 10:
            landed(0)
        if n == 11:
            to_p0[0].wait_recv()
            fill_lane(m_p0, p0, 0, 256)
        if n == 12:
            own_p0(0, 0)
    fill_lane(m_own, own, 256, 256)
    fill_row(mc_own, own, 256, 256)
    landed(1)
    own_own(0, 1)
    own_own(1, 0)
    own_own(1, 1)
    own_near(0, 0, 256)
    mated(0)
    mated(1)
    own_near(1, 0, 256)
    behind(0)
    behind(1)
    back_near(0, 256, 0, 256)
    own_p0(1, 0)
    to_p0[1].wait_recv()
    fill_lane(m_p0, p0, 256, 256)
    landed(2)
    own_p0(0, 1)
    own_p0(1, 1)
    own_near(0, 256, PART)
    behind(2)
    mated(2)
    own_near(1, 256, PART)
    back_near(0, 256, 256, PART)
    back_near(256, PART, 0, 256)
    back_near(256, PART, 256, PART)
    landed(3)
    own_near(0, 384, PART)
    behind(3)
    mated(3)
    back_near(384, PART, 0, 256)
    back_near(0, 256, 384, PART)
    back_near(256, 256, 384, PART)
    back_near(384, PART, 256, PART)

    def give_back(j, device):
        return pltpu.make_async_remote_copy(
            src_ref=ret_out.at[j],
            dst_ref=ret_in.at[j],
            send_sem=rs.at[j],
            recv_sem=rr.at[j],
            device_id=device,
            device_id_type=MESH,
        )

    backs = [give_back(0, up), give_back(1, up_mate), give_back(2, down)]

    def turned(racc):
        return dot_t(sum_row, racc[...], lax.Precision.HIGHEST)

    ret_out[2] = turned(r_back)
    backs[2].start()
    ret_out[0] = c_near[0]
    own_near(1, 384, PART)
    backs[0].start()
    ret_out[1] = c_near[1]
    total = turned(r_own)
    backs[1].start()
    for sent in backs:
        sent.wait_recv()
    for j in range(3):
        total = total + ret_in[j]
    total = jnp.sum(total, axis=0, keepdims=True)
    for j in range(4):
        fin_out[j] = total[:, j * PART : (j + 1) * PART]
    fin_in[0] = fin_out[0]

    def finish(r):
        dx, dy = TURNS[r]
        return pltpu.make_async_remote_copy(
            src_ref=fin_out.at[r // 4],
            dst_ref=fin_in.at[r],
            send_sem=fs.at[r],
            recv_sem=fr.at[r],
            device_id=plane(4 - dx, 4 - dy),
            device_id_type=MESH,
        )

    for r in range(15, 0, -1):
        finish(r).start()
    wanted = (slots == rank).astype(f32)
    chosen = jnp.concatenate(
        [(cluster == cluster_of(r)).astype(f32) for r in range(16)], axis=0
    )
    for r in range(1, 16):
        finish(r).wait_recv()
    sums = jnp.concatenate(
        [fin_in[r][:, (r % 4) * SLOT : (r % 4 + 1) * SLOT] for r in range(16)], axis=0
    )
    found = jnp.dot(sums, wanted, preferred_element_type=f32, precision=lax.Precision.HIGHEST)
    result[...] = jnp.sum(found * chosen, axis=0, keepdims=True)

    for r in range(16):
        if r:
            exchange(r).wait_send()
            finish(r).wait_send()
        to_near[r].wait_send()
        to_back[r].wait_send()
    for h in range(2):
        to_p0[h].wait_send()
    for g in range(4):
        to_mate[g].wait_send()
    for sent in backs:
        sent.wait_send()


def shards(embeddings, cluster_ids):
    dma = pltpu.SemaphoreType.DMA
    block = pltpu.VMEM((BLOCK, FEAT), bf16)
    racc = pltpu.VMEM((BLOCK, 128), f32)
    cacc = pltpu.VMEM((8, BLOCK), f32)
    soft = pl.pallas_call(
        kernel,
        out_shape=jax.ShapeDtypeStruct((1, ROWS), f32),
        in_specs=[
            pl.BlockSpec(memory_space=pltpu.HBM),
            pl.BlockSpec(memory_space=pltpu.VMEM),
        ],
        out_specs=pl.BlockSpec(memory_space=pltpu.VMEM),
        scratch_shapes=[
            pltpu.VMEM((ROWS, FEAT), bf16),
            pltpu.VMEM((ROWS, FEAT), bf16),
            block, block,
            pltpu.VMEM((2, BLOCK, FEAT), bf16),
            block, block,
            racc, racc,
            pltpu.VMEM((2, 8, BLOCK), f32),
            cacc, cacc,
            pltpu.VMEM((2, 8, BLOCK), f32),
            racc, racc,
            pltpu.VMEM((3, 8, BLOCK), f32),
            pltpu.VMEM((3, 8, BLOCK), f32),
            pltpu.VMEM((4, 1, PART), f32),
            pltpu.VMEM((16, 1, PART), f32),
            dma((4,)),
            dma((16,)), dma((16,)),
            dma((16,)), dma((16,)), dma((16,)), dma((16,)),
            dma((2,)), dma((2,)), dma((4,)), dma((4,)),
            dma((3,)), dma((3,)),
            dma((16,)), dma((16,)),
        ],
        compiler_params=pltpu.CompilerParams(
            collective_id=0, has_side_effects=True, vmem_limit_bytes=48 * 2**20
        ),
    )(embeddings, cluster_ids.reshape(1, ROWS))
    return jnp.log1p(soft.reshape(ROWS))


def solution(mesh):
    return jax.shard_map(
        shards,
        mesh=mesh,
        in_specs=(P(("grp", "blk"), None), P(("grp", "blk"))),
        out_specs=P(("grp", "blk")),
        check_vma=False,
    )
```

```python
import functools

import jax
import jax.numpy as jnp
from jax import lax
from jax.experimental import pallas as pl
from jax.experimental.pallas import tpu as pltpu
from jax.sharding import PartitionSpec as P

MESH = pl.DeviceIdType.MESH
ROWS = 256
FEAT = 1024
SLOT = 32
BLOCK = 16 * SLOT
PART = 4 * SLOT
TURNS = (
    (0, 0), (0, 1), (1, 0), (0, 3), (3, 0), (1, 1), (3, 3), (1, 3),
    (3, 1), (0, 2), (2, 0), (2, 1), (1, 2), (2, 3), (3, 2), (2, 2),
)
AHEAD = 5
LIMIT = 67043328
LOG2E = 1.4426950408889634
SCALE = -20.0 * LOG2E
SHIFT = 14.0 * LOG2E
MARK = 1.5
f32 = jnp.float32
bf16 = jnp.bfloat16


def dot_t(a, b, precision=None):
    return lax.dot_general(
        a, b, (((1,), (1,)), ((), ())), preferred_element_type=f32, precision=precision
    )


def kernel(
    emb_hbm, ids_hbm, result,
    emb, ids, unit, out, own, near, back, p0,
    r_own, r_back, c_near, m_own, m_p0, m_near, mc_own, mc_back,
    ret_out, ret_in, fin_out, fin_in,
    es, p1s, p1r, ns, nr, bs, br, p0s, p0r, xs, xr, rs, rr, fs, fr,
):
    x = lax.axis_index("grp")
    b = lax.axis_index("blk")
    z = b // 8
    y = lax.rem(b // 2, 4)
    k = lax.rem(b, 2)

    def at(xx, yy, zz, kk):
        return (xx, zz * 8 + yy * 2 + kk)

    z_up = lax.rem(z + 1, 4)
    z_down = lax.rem(z + 3, 4)
    up = at(x, y, z_up, k)
    down = at(x, y, z_down, k)
    up_mate = at(x, y, z_up, 1 - k)
    down_mate = at(x, y, z_down, 1 - k)
    mate = at(x, y, z, 1 - k)
    pick = z // 2

    def plane(dx, dy):
        return at(lax.rem(x + dx, 4), lax.rem(y + dy, 4), z, k)

    def piece(r, count=1):
        return pl.ds(r * SLOT, count * SLOT)

    barrier = pltpu.get_barrier_semaphore()
    peers = [plane(r // 4, r % 4) for r in range(1, 16)] + [
        up, down, mate, up_mate, down_mate
    ]
    fetches = [
        pltpu.make_async_copy(
            emb_hbm.at[pl.ds(c * 64, 64), :], emb.at[pl.ds(c * 64, 64), :], es.at[c]
        )
        for c in range(4)
    ]
    fetch_ids = pltpu.make_async_copy(ids_hbm, ids, es.at[4])
    fetch_ids.start()
    for fetch in fetches:
        fetch.start()
    for peer in peers:
        pl.semaphore_signal(barrier, inc=1, device_id=peer, device_id_type=MESH)

    for c in range(4):
        rows = pl.ds(c * 64, 64)
        fetches[c].wait()
        wide = emb[rows, :].astype(f32)
        squared = jnp.sum(wide * wide, axis=1, keepdims=True) + 1e-06
        unit[rows, :] = (wide * lax.rsqrt(squared)).astype(bf16)
    fetch_ids.wait()
    cluster = ids[...]
    hot = (cluster == lax.broadcasted_iota(jnp.int32, (16, ROWS), 0)).astype(f32)
    before = (
        lax.broadcasted_iota(jnp.int32, (ROWS, ROWS), 0)
        < lax.broadcasted_iota(jnp.int32, (ROWS, ROWS), 1)
    ).astype(f32).astype(bf16)
    ranks = jnp.dot(hot.astype(bf16), before, preferred_element_type=f32)
    rank = jnp.sum(hot * ranks, axis=0, keepdims=True).astype(jnp.int32)
    position = cluster * SLOT + rank
    first_lane = lax.broadcasted_iota(jnp.int32, (PART, 128), 1) == 0

    def exchange(r):
        return pltpu.make_async_remote_copy(
            src_ref=out.at[piece(r), :],
            dst_ref=own.at[piece(r), :],
            send_sem=p1s.at[r],
            recv_sem=p1r.at[r],
            device_id=plane(*TURNS[r]),
            device_id_type=MESH,
        )

    def cluster_of(r):
        dx, dy = TURNS[r]
        return lax.rem(x + dx, 4) * 4 + lax.rem(y + dy, 4)

    slots = lax.broadcasted_iota(jnp.int32, (SLOT, ROWS), 0)
    for g in range(4):
        placed = jnp.concatenate(
            [
                (slots + cluster_of(r) * SLOT == position).astype(f32)
                for r in range(4 * g, 4 * g + 4)
            ],
            axis=0,
        )
        empty = jnp.sum(placed, axis=1, keepdims=True) < 0.5
        placed = placed.astype(bf16)
        for c in range(4):
            cols = pl.ds(c * 256, 256)
            moved = jnp.dot(placed, unit[:, cols], preferred_element_type=f32)
            if c == 0:
                head = jnp.where(first_lane & empty, MARK, moved[:, :128])
                moved = jnp.concatenate([head, moved[:, 128:]], axis=1)
            moved = moved.astype(bf16)
            if g == 0:
                own[piece(0), cols] = moved[:SLOT, :]
            out[piece(4 * g, 4), cols] = moved

    pl.semaphore_wait(barrier, len(peers))
    for r in range(1, 1 + AHEAD):
        exchange(r).start()

    for sums in (r_own, r_back, c_near):
        sums[...] = jnp.zeros_like(sums)

    def pass_on(r, src, dst, send, recv, device):
        return pltpu.make_async_remote_copy(
            src_ref=src.at[piece(r), :],
            dst_ref=dst.at[piece(r), :],
            send_sem=send.at[r],
            recv_sem=recv.at[r],
            device_id=device,
            device_id_type=MESH,
        )

    def share(n, size, src, dst, send, recv):
        rows = pl.ds(n * size, size)
        return pltpu.make_async_remote_copy(
            src_ref=src.at[rows, :],
            dst_ref=dst.at[rows, :],
            send_sem=send.at[n],
            recv_sem=recv.at[n],
            device_id=mate,
            device_id_type=MESH,
        )

    to_near = [pass_on(r, own, near.at[0], ns, nr, down) for r in range(16)]
    to_back = [pass_on(r, own, back, bs, br, up) for r in range(16)]
    to_p0 = [share(h, 256, own, p0, p0s, p0r) for h in range(2)]
    to_mate = [share(g, PART, near.at[0], near.at[1], xs, xr) for g in range(4)]

    pick_row = (lax.broadcasted_iota(jnp.int32, (8, 128), 1) == 0).astype(f32).astype(bf16)
    pick_col = (lax.broadcasted_iota(jnp.int32, (128, 128), 0) == 0).astype(f32).astype(bf16)
    sum_row = (lax.broadcasted_iota(jnp.int32, (8, 128), 0) == 0).astype(f32)

    def lane_mask(block):
        return jnp.where(dot_t(pick_row, block[:, :128]) > 1.25, 0.0, 1.0)

    def row_mask(block):
        marks = jnp.dot(block[:, :128], pick_col, preferred_element_type=f32)
        return jnp.where(marks > 1.25, 0.0, 1.0)

    def meet(
        left, l0, height, right, r0, width, mask, racc,
        cacc=None, cmask=None, diagonal=False,
    ):
        similar = dot_t(left[pl.ds(l0, height), :], right[pl.ds(r0, width), :])
        total = jnp.zeros((8, width), f32)
        for c in range(height // 32):
            block = similar[c * 32 : (c + 1) * 32, :]
            w = 1.0 / (1.0 + jnp.exp2(block * SCALE + SHIFT))
            if diagonal:
                here = l0 + c * 32 + lax.broadcasted_iota(jnp.int32, (32, width), 0)
                there = r0 + lax.broadcasted_iota(jnp.int32, (32, width), 1)
                w = jnp.where(here == there, 0.0, w)
            rows = pl.ds(l0 + c * 32, 32)
            wr = w * mask[0:1, pl.ds(r0, width)]
            if width == 256:
                wr = wr[:, :128] + wr[:, 128:]
            racc[rows, :] += wr
            if cacc is not None:
                cm = cmask[rows, :]
                if width == 256:
                    cm = jnp.concatenate([cm, cm], axis=1)
                wc = w * cm
                total = total + wc[0:8] + wc[8:16] + wc[16:24] + wc[24:32]
        if cacc is not None:
            cacc[:, pl.ds(r0, width)] += total

    def fill_lane(mask, block, r0, size):
        rows = pl.ds(r0, size)
        mask[:, rows] = lane_mask(block[rows, :128])

    def fill_row(mask, block, r0, size):
        rows = pl.ds(r0, size)
        mask[rows, :] = row_mask(block[rows, :128])

    def own_own(l, h):
        meet(own, l * 256, 256, own, h * 256, 256, m_own, r_own, diagonal=l == h)

    def own_p0(l, h):
        meet(own, l * 256, 256, p0, h * 256, 256, m_p0, r_own)

    def own_near(j, r0, width):
        meet(
            own, 0, BLOCK, near.at[j], r0, width, m_near.at[j], r_own,
            c_near.at[j], mc_own,
        )

    def back_near(l0, height, r0, width):
        meet(
            back, l0, height, near.at[pick], r0, width, m_near.at[pick], r_back,
            c_near.at[pick], mc_back,
        )

    def landed(g):
        for r in range(4 * g, 4 * g + 4):
            to_near[r].wait_recv()
        to_mate[g].start()
        fill_lane(m_near.at[0], near.at[0], g * PART, PART)

    def behind(g):
        for r in range(4 * g, 4 * g + 4):
            to_back[r].wait_recv()
        fill_row(mc_back, back, g * PART, PART)

    def mated(g):
        to_mate[g].wait_recv()
        fill_lane(m_near.at[1], near.at[1], g * PART, PART)

    for n in range(16):
        if n:
            exchange(n).wait_recv()
        if n + AHEAD + 1 < 16:
            exchange(n + AHEAD + 1).start()
        to_near[n].start()
        to_back[n].start()
        if n % 8 == 7:
            to_p0[n // 8].start()
        if n == 8:
            fill_lane(m_own, own, 0, 256)
            fill_row(mc_own, own, 0, 256)
        if n == 9:
            own_own(0, 0)
        if n == 10:
            landed(0)
        if n == 11:
            to_p0[0].wait_recv()
            fill_lane(m_p0, p0, 0, 256)
        if n == 12:
            own_p0(0, 0)
    fill_lane(m_own, own, 256, 256)
    fill_row(mc_own, own, 256, 256)
    landed(1)
    own_own(0, 1)
    own_own(1, 0)
    own_own(1, 1)
    own_near(0, 0, 256)
    mated(0)
    mated(1)
    own_near(1, 0, 256)
    behind(0)
    behind(1)
    back_near(0, 256, 0, 256)
    own_p0(1, 0)
    to_p0[1].wait_recv()
    fill_lane(m_p0, p0, 256, 256)
    landed(2)
    own_p0(0, 1)
    own_p0(1, 1)
    own_near(0, 256, PART)
    behind(2)
    mated(2)
    own_near(1, 256, PART)
    back_near(0, 384, 256, PART)
    back_near(256, PART, 0, 256)
    landed(3)
    own_near(0, 384, PART)
    behind(3)
    mated(3)
    back_near(0, BLOCK, 384, PART)
    back_near(384, PART, 0, 256)
    back_near(384, PART, 256, PART)

    def give_back(j, device):
        return pltpu.make_async_remote_copy(
            src_ref=ret_out.at[j],
            dst_ref=ret_in.at[j],
            send_sem=rs.at[j],
            recv_sem=rr.at[j],
            device_id=device,
            device_id_type=MESH,
        )

    backs = [give_back(0, up), give_back(1, up_mate), give_back(2, down)]

    def turned(racc):
        return dot_t(sum_row, racc[...], lax.Precision.HIGHEST)

    ret_out[2] = turned(r_back)
    backs[2].start()
    ret_out[0] = c_near[0]
    own_near(1, 384, PART)
    backs[0].start()
    ret_out[1] = c_near[1]
    total = turned(r_own)
    backs[1].start()
    for sent in backs:
        sent.wait_recv()
    for j in range(3):
        total = total + ret_in[j]
    total = jnp.sum(total, axis=0, keepdims=True)
    for j in range(4):
        fin_out[j] = total[:, j * PART : (j + 1) * PART]
    fin_in[0] = fin_out[0]

    def finish(r):
        dx, dy = TURNS[r]
        return pltpu.make_async_remote_copy(
            src_ref=fin_out.at[r // 4],
            dst_ref=fin_in.at[r],
            send_sem=fs.at[r],
            recv_sem=fr.at[r],
            device_id=plane(4 - dx, 4 - dy),
            device_id_type=MESH,
        )

    for r in range(15, 0, -1):
        finish(r).start()
    wanted = (slots == rank).astype(f32)
    chosen = jnp.concatenate(
        [(cluster == cluster_of(r)).astype(f32) for r in range(16)], axis=0
    )
    for r in range(1, 16):
        finish(r).wait_recv()
    sums = jnp.concatenate(
        [fin_in[r][:, (r % 4) * SLOT : (r % 4 + 1) * SLOT] for r in range(16)], axis=0
    )
    found = jnp.dot(sums, wanted, preferred_element_type=f32, precision=lax.Precision.HIGHEST)
    result[...] = jnp.sum(found * chosen, axis=0, keepdims=True)

    for r in range(16):
        if r:
            exchange(r).wait_send()
            finish(r).wait_send()
        to_near[r].wait_send()
        to_back[r].wait_send()
    for h in range(2):
        to_p0[h].wait_send()
    for g in range(4):
        to_mate[g].wait_send()
    for sent in backs:
        sent.wait_send()


def shards(embeddings, cluster_ids):
    dma = pltpu.SemaphoreType.DMA
    block = pltpu.VMEM((BLOCK, FEAT), bf16)
    racc = pltpu.VMEM((BLOCK, 128), f32)
    cacc = pltpu.VMEM((8, BLOCK), f32)
    soft = pl.pallas_call(
        kernel,
        out_shape=jax.ShapeDtypeStruct((1, ROWS), f32),
        in_specs=[pl.BlockSpec(memory_space=pltpu.HBM)] * 2,
        out_specs=pl.BlockSpec(memory_space=pltpu.VMEM),
        scratch_shapes=[
            pltpu.VMEM((ROWS, FEAT), bf16),
            pltpu.VMEM((1, ROWS), jnp.int32),
            pltpu.VMEM((ROWS, FEAT), bf16),
            block, block,
            pltpu.VMEM((2, BLOCK, FEAT), bf16),
            block, block,
            racc, racc,
            pltpu.VMEM((2, 8, BLOCK), f32),
            cacc, cacc,
            pltpu.VMEM((2, 8, BLOCK), f32),
            racc, racc,
            pltpu.VMEM((3, 8, BLOCK), f32),
            pltpu.VMEM((3, 8, BLOCK), f32),
            pltpu.VMEM((4, 1, PART), f32),
            pltpu.VMEM((16, 1, PART), f32),
            dma((5,)),
            dma((16,)), dma((16,)),
            dma((16,)), dma((16,)), dma((16,)), dma((16,)),
            dma((2,)), dma((2,)), dma((4,)), dma((4,)),
            dma((3,)), dma((3,)),
            dma((16,)), dma((16,)),
        ],
        compiler_params=pltpu.CompilerParams(
            collective_id=0, has_side_effects=True, vmem_limit_bytes=LIMIT
        ),
    )(embeddings, cluster_ids.reshape(1, ROWS))
    return jnp.log1p(soft.reshape(ROWS))


def solution(mesh):
    return jax.shard_map(
        shards,
        mesh=mesh,
        in_specs=(P(("grp", "blk"), None), P(("grp", "blk"))),
        out_specs=P(("grp", "blk")),
        check_vma=False,
    )
```

```python
import functools

import jax
import jax.numpy as jnp
from jax import lax
from jax.experimental import pallas as pl
from jax.experimental.pallas import tpu as pltpu
from jax.sharding import PartitionSpec as P

MESH = pl.DeviceIdType.MESH
ROWS = 256
FEAT = 1024
SLOT = 32
BLOCK = 16 * SLOT
PART = 4 * SLOT
TURNS = (
    (0, 0), (0, 1), (1, 0), (0, 3), (3, 0), (1, 1), (3, 3), (1, 3),
    (3, 1), (0, 2), (2, 0), (2, 1), (1, 2), (2, 3), (3, 2), (2, 2),
)
AHEAD = 8
LIMIT = 67043328
LOG2E = 1.4426950408889634
SCALE = -20.0 * LOG2E
SHIFT = 14.0 * LOG2E
MARK = 1.5
f32 = jnp.float32
bf16 = jnp.bfloat16


def dot_t(a, b, precision=None):
    return lax.dot_general(
        a, b, (((1,), (1,)), ((), ())), preferred_element_type=f32, precision=precision
    )


def kernel(
    emb_hbm, ids_hbm, result,
    emb, ids, unit, out, own, near, back, p0,
    r_own, r_back, c_near, m_own, m_p0, m_near, mc_own, mc_back,
    ret_out, ret_in, fin_out, fin_in,
    es, p1s, p1r, ns, nr, bs, br, p0s, p0r, xs, xr, rs, rr, fs, fr,
):
    x = lax.axis_index("grp")
    b = lax.axis_index("blk")
    z = b // 8
    y = lax.rem(b // 2, 4)
    k = lax.rem(b, 2)

    def at(xx, yy, zz, kk):
        return (xx, zz * 8 + yy * 2 + kk)

    z_up = lax.rem(z + 1, 4)
    z_down = lax.rem(z + 3, 4)
    up = at(x, y, z_up, k)
    down = at(x, y, z_down, k)
    up_mate = at(x, y, z_up, 1 - k)
    down_mate = at(x, y, z_down, 1 - k)
    mate = at(x, y, z, 1 - k)
    pick = z // 2

    def plane(dx, dy):
        return at(lax.rem(x + dx, 4), lax.rem(y + dy, 4), z, k)

    def piece(r, count=1):
        return pl.ds(r * SLOT, count * SLOT)

    barrier = pltpu.get_barrier_semaphore()
    peers = [plane(r // 4, r % 4) for r in range(1, 16)] + [
        up, down, mate, up_mate, down_mate
    ]
    fetches = [
        pltpu.make_async_copy(
            emb_hbm.at[pl.ds(c * 64, 64), :], emb.at[pl.ds(c * 64, 64), :], es.at[c]
        )
        for c in range(4)
    ]
    fetch_ids = pltpu.make_async_copy(ids_hbm, ids, es.at[4])
    fetch_ids.start()
    for fetch in fetches:
        fetch.start()
    for peer in peers:
        pl.semaphore_signal(barrier, inc=1, device_id=peer, device_id_type=MESH)

    for c in range(4):
        rows = pl.ds(c * 64, 64)
        fetches[c].wait()
        wide = emb[rows, :].astype(f32)
        squared = jnp.sum(wide * wide, axis=1, keepdims=True) + 1e-06
        unit[rows, :] = (wide * lax.rsqrt(squared)).astype(bf16)
    fetch_ids.wait()
    cluster = ids[...]
    hot = (cluster == lax.broadcasted_iota(jnp.int32, (16, ROWS), 0)).astype(f32)
    before = (
        lax.broadcasted_iota(jnp.int32, (ROWS, ROWS), 0)
        < lax.broadcasted_iota(jnp.int32, (ROWS, ROWS), 1)
    ).astype(f32).astype(bf16)
    ranks = jnp.dot(hot.astype(bf16), before, preferred_element_type=f32)
    rank = jnp.sum(hot * ranks, axis=0, keepdims=True).astype(jnp.int32)
    position = cluster * SLOT + rank
    first_lane = lax.broadcasted_iota(jnp.int32, (PART, 128), 1) == 0

    def exchange(r):
        return pltpu.make_async_remote_copy(
            src_ref=out.at[piece(r), :],
            dst_ref=own.at[piece(r), :],
            send_sem=p1s.at[r],
            recv_sem=p1r.at[r],
            device_id=plane(*TURNS[r]),
            device_id_type=MESH,
        )

    def cluster_of(r):
        dx, dy = TURNS[r]
        return lax.rem(x + dx, 4) * 4 + lax.rem(y + dy, 4)

    slots = lax.broadcasted_iota(jnp.int32, (SLOT, ROWS), 0)
    for g in range(4):
        placed = jnp.concatenate(
            [
                (slots + cluster_of(r) * SLOT == position).astype(f32)
                for r in range(4 * g, 4 * g + 4)
            ],
            axis=0,
        )
        empty = jnp.sum(placed, axis=1, keepdims=True) < 0.5
        placed = placed.astype(bf16)
        for c in range(4):
            cols = pl.ds(c * 256, 256)
            moved = jnp.dot(placed, unit[:, cols], preferred_element_type=f32)
            if c == 0:
                head = jnp.where(first_lane & empty, MARK, moved[:, :128])
                moved = jnp.concatenate([head, moved[:, 128:]], axis=1)
            moved = moved.astype(bf16)
            if g == 0:
                own[piece(0), cols] = moved[:SLOT, :]
            out[piece(4 * g, 4), cols] = moved

    pl.semaphore_wait(barrier, len(peers))
    for r in range(1, 1 + AHEAD):
        exchange(r).start()

    for sums in (r_own, r_back, c_near):
        sums[...] = jnp.zeros_like(sums)

    def pass_on(r, src, dst, send, recv, device):
        return pltpu.make_async_remote_copy(
            src_ref=src.at[piece(r), :],
            dst_ref=dst.at[piece(r), :],
            send_sem=send.at[r],
            recv_sem=recv.at[r],
            device_id=device,
            device_id_type=MESH,
        )

    def share(n, size, src, dst, send, recv):
        rows = pl.ds(n * size, size)
        return pltpu.make_async_remote_copy(
            src_ref=src.at[rows, :],
            dst_ref=dst.at[rows, :],
            send_sem=send.at[n],
            recv_sem=recv.at[n],
            device_id=mate,
            device_id_type=MESH,
        )

    to_near = [pass_on(r, own, near.at[0], ns, nr, down) for r in range(16)]
    to_back = [pass_on(r, own, back, bs, br, up) for r in range(16)]
    to_p0 = [share(h, 256, own, p0, p0s, p0r) for h in range(2)]
    to_mate = [share(g, PART, near.at[0], near.at[1], xs, xr) for g in range(4)]

    pick_row = (lax.broadcasted_iota(jnp.int32, (8, 128), 1) == 0).astype(f32).astype(bf16)
    pick_col = (lax.broadcasted_iota(jnp.int32, (128, 128), 0) == 0).astype(f32).astype(bf16)
    sum_row = (lax.broadcasted_iota(jnp.int32, (8, 128), 0) == 0).astype(f32).astype(bf16)

    def lane_mask(block):
        return jnp.where(dot_t(pick_row, block[:, :128]) > 1.25, 0.0, 1.0)

    def row_mask(block):
        marks = jnp.dot(block[:, :128], pick_col, preferred_element_type=f32)
        return jnp.where(marks > 1.25, 0.0, 1.0)

    def meet(
        left, l0, height, right, r0, width, mask, racc,
        cacc=None, cmask=None, diagonal=False, rows_of=None,
    ):
        if rows_of is None:
            rows_of = right[pl.ds(r0, width), :]
            allowed = mask[0:1, pl.ds(r0, width)]
        else:
            allowed = mask
        similar = dot_t(left[pl.ds(l0, height), :], rows_of)
        total = jnp.zeros((8, width), f32)
        for c in range(height // 32):
            block = similar[c * 32 : (c + 1) * 32, :]
            w = 1.0 / (1.0 + jnp.exp2(block * SCALE + SHIFT))
            if diagonal:
                here = l0 + c * 32 + lax.broadcasted_iota(jnp.int32, (32, width), 0)
                there = r0 + lax.broadcasted_iota(jnp.int32, (32, width), 1)
                w = jnp.where(here == there, 0.0, w)
            rows = pl.ds(l0 + c * 32, 32)
            wr = w * allowed
            if width == 256:
                wr = wr[:, :128] + wr[:, 128:]
            racc[rows, :] += wr
            if cacc is not None:
                cm = cmask[rows, :]
                if width == 256:
                    cm = jnp.concatenate([cm, cm], axis=1)
                wc = w * cm
                total = total + wc[0:8] + wc[8:16] + wc[16:24] + wc[24:32]
        if right is None:
            cacc[0, :, pl.ds(r0, PART)] += total[:, :PART]
            cacc[1, :, pl.ds(r0, PART)] += total[:, PART:]
        elif cacc is not None:
            cacc[:, pl.ds(r0, width)] += total

    def fill_lane(mask, block, r0, size):
        rows = pl.ds(r0, size)
        mask[:, rows] = lane_mask(block[rows, :128])

    def fill_row(mask, block, r0, size):
        rows = pl.ds(r0, size)
        mask[rows, :] = row_mask(block[rows, :128])

    def own_own(l, h):
        meet(own, l * 256, 256, own, h * 256, 256, m_own, r_own, diagonal=l == h)

    def own_p0(l, h):
        meet(own, l * 256, 256, p0, h * 256, 256, m_p0, r_own)

    def own_near(j, r0, width):
        for l0 in (0, 256):
            meet(
                own, l0, 256, near.at[j], r0, width, m_near.at[j], r_own,
                c_near.at[j], mc_own,
            )

    def own_both(r0):
        cols = pl.ds(r0, PART)
        rows_of = jnp.concatenate([near[0, cols, :], near[1, cols, :]], axis=0)
        allowed = jnp.concatenate([m_near[0, 0:1, cols], m_near[1, 0:1, cols]], axis=1)
        for l0 in (0, 256):
            meet(
                own, l0, 256, None, r0, 256, allowed, r_own,
                c_near, mc_own, rows_of=rows_of,
            )

    def back_near(l0, height, r0, width):
        meet(
            back, l0, height, near.at[pick], r0, width, m_near.at[pick], r_back,
            c_near.at[pick], mc_back,
        )

    def landed(g):
        for r in range(4 * g, 4 * g + 4):
            to_near[r].wait_recv()
        to_mate[g].start()
        fill_lane(m_near.at[0], near.at[0], g * PART, PART)

    def behind(g):
        for r in range(4 * g, 4 * g + 4):
            to_back[r].wait_recv()
        fill_row(mc_back, back, g * PART, PART)

    def mated(g):
        to_mate[g].wait_recv()
        fill_lane(m_near.at[1], near.at[1], g * PART, PART)

    for n in range(16):
        if n:
            exchange(n).wait_recv()
        if n + AHEAD + 1 < 16:
            exchange(n + AHEAD + 1).start()
        to_near[n].start()
        to_back[n].start()
        if n % 8 == 7:
            to_p0[n // 8].start()
        if n == 8:
            fill_lane(m_own, own, 0, 256)
            fill_row(mc_own, own, 0, 256)
        if n == 9:
            own_own(0, 0)
        if n == 10:
            landed(0)
        if n == 11:
            to_p0[0].wait_recv()
            fill_lane(m_p0, p0, 0, 256)
        if n == 12:
            own_p0(0, 0)
    fill_lane(m_own, own, 256, 256)
    fill_row(mc_own, own, 256, 256)
    landed(1)
    own_own(0, 1)
    own_own(1, 0)
    own_own(1, 1)
    own_near(0, 0, 256)
    mated(0)
    mated(1)
    own_near(1, 0, 256)
    behind(0)
    behind(1)
    back_near(0, 256, 0, 256)
    to_p0[1].wait_recv()
    fill_lane(m_p0, p0, 256, 256)
    landed(2)
    behind(2)
    back_near(256, PART, 0, 256)
    mated(2)
    own_both(256)
    back_near(0, 256, 256, PART)
    back_near(256, PART, 256, PART)
    landed(3)
    behind(3)
    back_near(384, PART, 0, 256)
    back_near(384, PART, 256, PART)
    mated(3)
    back_near(0, 256, 384, PART)
    back_near(256, 256, 384, PART)

    def give_back(j, device):
        return pltpu.make_async_remote_copy(
            src_ref=ret_out.at[j],
            dst_ref=ret_in.at[j],
            send_sem=rs.at[j],
            recv_sem=rr.at[j],
            device_id=device,
            device_id_type=MESH,
        )

    backs = [give_back(0, up), give_back(1, up_mate), give_back(2, down)]

    def turned(racc):
        left = racc[...]
        done = jnp.zeros((8, BLOCK), f32)
        for _ in range(3):
            part = left.astype(bf16)
            left = left - part.astype(f32)
            done = done + dot_t(sum_row, part)
        return done

    ret_out[2] = turned(r_back)
    backs[2].start()
    own_both(384)
    ret_out[0] = c_near[0]
    backs[0].start()
    ret_out[1] = c_near[1]
    backs[1].start()
    own_p0(1, 0)
    own_p0(0, 1)
    own_p0(1, 1)
    total = turned(r_own)
    for sent in backs:
        sent.wait_recv()
    for j in range(3):
        total = total + ret_in[j]
    total = jnp.sum(total, axis=0, keepdims=True)
    for j in range(4):
        fin_out[j] = total[:, j * PART : (j + 1) * PART]
    fin_in[0] = fin_out[0]

    def finish(r):
        dx, dy = TURNS[r]
        return pltpu.make_async_remote_copy(
            src_ref=fin_out.at[r // 4],
            dst_ref=fin_in.at[r],
            send_sem=fs.at[r],
            recv_sem=fr.at[r],
            device_id=plane(4 - dx, 4 - dy),
            device_id_type=MESH,
        )

    for r in range(15, 0, -1):
        finish(r).start()
    wanted = (slots == rank).astype(f32)
    chosen = jnp.concatenate(
        [(cluster == cluster_of(r)).astype(f32) for r in range(16)], axis=0
    )
    for r in range(1, 16):
        finish(r).wait_recv()
    sums = jnp.concatenate(
        [fin_in[r][:, (r % 4) * SLOT : (r % 4 + 1) * SLOT] for r in range(16)], axis=0
    )
    found = jnp.dot(sums, wanted, preferred_element_type=f32, precision=lax.Precision.HIGHEST)
    result[...] = jnp.sum(found * chosen, axis=0, keepdims=True)

    for r in range(16):
        if r:
            exchange(r).wait_send()
            finish(r).wait_send()
        to_near[r].wait_send()
        to_back[r].wait_send()
    for h in range(2):
        to_p0[h].wait_send()
    for g in range(4):
        to_mate[g].wait_send()
    for sent in backs:
        sent.wait_send()


def shards(embeddings, cluster_ids):
    dma = pltpu.SemaphoreType.DMA
    block = pltpu.VMEM((BLOCK, FEAT), bf16)
    racc = pltpu.VMEM((BLOCK, 128), f32)
    cacc = pltpu.VMEM((8, BLOCK), f32)
    soft = pl.pallas_call(
        kernel,
        out_shape=jax.ShapeDtypeStruct((1, ROWS), f32),
        in_specs=[pl.BlockSpec(memory_space=pltpu.HBM)] * 2,
        out_specs=pl.BlockSpec(memory_space=pltpu.VMEM),
        scratch_shapes=[
            pltpu.VMEM((ROWS, FEAT), bf16),
            pltpu.VMEM((1, ROWS), jnp.int32),
            pltpu.VMEM((ROWS, FEAT), bf16),
            block, block,
            pltpu.VMEM((2, BLOCK, FEAT), bf16),
            block, block,
            racc, racc,
            pltpu.VMEM((2, 8, BLOCK), f32),
            cacc, cacc,
            pltpu.VMEM((2, 8, BLOCK), f32),
            racc, racc,
            pltpu.VMEM((3, 8, BLOCK), f32),
            pltpu.VMEM((3, 8, BLOCK), f32),
            pltpu.VMEM((4, 1, PART), f32),
            pltpu.VMEM((16, 1, PART), f32),
            dma((5,)),
            dma((16,)), dma((16,)),
            dma((16,)), dma((16,)), dma((16,)), dma((16,)),
            dma((2,)), dma((2,)), dma((4,)), dma((4,)),
            dma((3,)), dma((3,)),
            dma((16,)), dma((16,)),
        ],
        compiler_params=pltpu.CompilerParams(
            collective_id=0, has_side_effects=True, vmem_limit_bytes=LIMIT
        ),
    )(embeddings, cluster_ids.reshape(1, ROWS))
    return jnp.log1p(soft.reshape(ROWS))


def solution(mesh):
    return jax.shard_map(
        shards,
        mesh=mesh,
        in_specs=(P(("grp", "blk"), None), P(("grp", "blk"))),
        out_specs=P(("grp", "blk")),
        check_vma=False,
    )
```

```python
import functools

import jax
import jax.numpy as jnp
from jax import lax
from jax.experimental import pallas as pl
from jax.experimental.pallas import tpu as pltpu
from jax.sharding import PartitionSpec as P

MESH = pl.DeviceIdType.MESH
ROWS = 256
FEAT = 1024
SLOT = 32
BLOCK = 16 * SLOT
PART = 4 * SLOT
TURNS = (
    (0, 0), (0, 1), (1, 0), (0, 3), (3, 0), (1, 1), (3, 3), (1, 3),
    (3, 1), (0, 2), (2, 0), (2, 1), (1, 2), (2, 3), (3, 2), (2, 2),
)
AHEAD = 8
LIMIT = 67043328
LOG2E = 1.4426950408889634
SCALE = -20.0 * LOG2E
SHIFT = 14.0 * LOG2E
MARK = 1.5
f32 = jnp.float32
bf16 = jnp.bfloat16


def dot_t(a, b, precision=None):
    return lax.dot_general(
        a, b, (((1,), (1,)), ((), ())), preferred_element_type=f32, precision=precision
    )


def kernel(
    emb_hbm, ids_hbm, result,
    emb, ids, unit, out, own, near, back, p0,
    r_own, r_back, c_near, m_own, m_p0, m_near, mc_own, mc_back,
    ret_out, ret_in, fin_out, fin_in,
    es, p1s, p1r, ns, nr, bs, br, p0s, p0r, xs, xr, rs, rr, fs, fr,
):
    x = lax.axis_index("grp")
    b = lax.axis_index("blk")
    z = b // 8
    y = lax.rem(b // 2, 4)
    k = lax.rem(b, 2)

    def at(xx, yy, zz, kk):
        return (xx, zz * 8 + yy * 2 + kk)

    z_up = lax.rem(z + 1, 4)
    z_down = lax.rem(z + 3, 4)
    up = at(x, y, z_up, k)
    down = at(x, y, z_down, k)
    up_mate = at(x, y, z_up, 1 - k)
    down_mate = at(x, y, z_down, 1 - k)
    mate = at(x, y, z, 1 - k)
    pick = z // 2

    def plane(dx, dy):
        return at(lax.rem(x + dx, 4), lax.rem(y + dy, 4), z, k)

    def piece(r, count=1):
        return pl.ds(r * SLOT, count * SLOT)

    barrier = pltpu.get_barrier_semaphore()
    peers = [plane(r // 4, r % 4) for r in range(1, 16)] + [
        up, down, mate, up_mate, down_mate
    ]
    fetches = [
        pltpu.make_async_copy(
            emb_hbm.at[pl.ds(c * 64, 64), :], emb.at[pl.ds(c * 64, 64), :], es.at[c]
        )
        for c in range(4)
    ]
    fetch_ids = pltpu.make_async_copy(ids_hbm, ids, es.at[4])
    fetch_ids.start()
    for fetch in fetches:
        fetch.start()
    for peer in peers:
        pl.semaphore_signal(barrier, inc=1, device_id=peer, device_id_type=MESH)

    for c in range(4):
        rows = pl.ds(c * 64, 64)
        fetches[c].wait()
        wide = emb[rows, :].astype(f32)
        squared = jnp.sum(wide * wide, axis=1, keepdims=True) + 1e-06
        unit[rows, :] = (wide * lax.rsqrt(squared)).astype(bf16)
    fetch_ids.wait()
    cluster = ids[...]
    hot = (cluster == lax.broadcasted_iota(jnp.int32, (16, ROWS), 0)).astype(f32)
    before = (
        lax.broadcasted_iota(jnp.int32, (ROWS, ROWS), 0)
        < lax.broadcasted_iota(jnp.int32, (ROWS, ROWS), 1)
    ).astype(f32).astype(bf16)
    ranks = jnp.dot(hot.astype(bf16), before, preferred_element_type=f32)
    rank = jnp.sum(hot * ranks, axis=0, keepdims=True).astype(jnp.int32)
    position = cluster * SLOT + rank
    first_lane = lax.broadcasted_iota(jnp.int32, (PART, 128), 1) == 0

    def exchange(r):
        return pltpu.make_async_remote_copy(
            src_ref=out.at[piece(r), :],
            dst_ref=own.at[piece(r), :],
            send_sem=p1s.at[r],
            recv_sem=p1r.at[r],
            device_id=plane(*TURNS[r]),
            device_id_type=MESH,
        )

    def cluster_of(r):
        dx, dy = TURNS[r]
        return lax.rem(x + dx, 4) * 4 + lax.rem(y + dy, 4)

    slots = lax.broadcasted_iota(jnp.int32, (SLOT, ROWS), 0)
    for g in range(4):
        placed = jnp.concatenate(
            [
                (slots + cluster_of(r) * SLOT == position).astype(f32)
                for r in range(4 * g, 4 * g + 4)
            ],
            axis=0,
        )
        empty = jnp.sum(placed, axis=1, keepdims=True) < 0.5
        placed = placed.astype(bf16)
        for c in range(4):
            cols = pl.ds(c * 256, 256)
            moved = jnp.dot(placed, unit[:, cols], preferred_element_type=f32)
            if c == 0:
                head = jnp.where(first_lane & empty, MARK, moved[:, :128])
                moved = jnp.concatenate([head, moved[:, 128:]], axis=1)
            moved = moved.astype(bf16)
            if g == 0:
                own[piece(0), cols] = moved[:SLOT, :]
            out[piece(4 * g, 4), cols] = moved

    pl.semaphore_wait(barrier, len(peers))
    for r in range(1, 1 + AHEAD):
        exchange(r).start()

    for sums in (r_own, r_back, c_near):
        sums[...] = jnp.zeros_like(sums)

    def pass_on(r, src, dst, send, recv, device):
        return pltpu.make_async_remote_copy(
            src_ref=src.at[piece(r), :],
            dst_ref=dst.at[piece(r), :],
            send_sem=send.at[r],
            recv_sem=recv.at[r],
            device_id=device,
            device_id_type=MESH,
        )

    def share(n, size, src, dst, send, recv):
        rows = pl.ds(n * size, size)
        return pltpu.make_async_remote_copy(
            src_ref=src.at[rows, :],
            dst_ref=dst.at[rows, :],
            send_sem=send.at[n],
            recv_sem=recv.at[n],
            device_id=mate,
            device_id_type=MESH,
        )

    to_near = [pass_on(r, own, near.at[0], ns, nr, down) for r in range(16)]
    to_back = [pass_on(r, own, back, bs, br, up) for r in range(16)]
    to_p0 = [share(h, 256, own, p0, p0s, p0r) for h in range(2)]
    to_mate = [share(g, PART, near.at[0], near.at[1], xs, xr) for g in range(4)]

    pick_row = (lax.broadcasted_iota(jnp.int32, (8, 128), 1) == 0).astype(f32).astype(bf16)
    pick_col = (lax.broadcasted_iota(jnp.int32, (128, 128), 0) == 0).astype(f32).astype(bf16)
    sum_row = (lax.broadcasted_iota(jnp.int32, (8, 128), 0) == 0).astype(f32).astype(bf16)

    def lane_mask(block):
        return jnp.where(dot_t(pick_row, block[:, :128]) > 1.25, 0.0, 1.0)

    def row_mask(block):
        marks = jnp.dot(block[:, :128], pick_col, preferred_element_type=f32)
        return jnp.where(marks > 1.25, 0.0, 1.0)

    def meet(
        left, l0, height, right, r0, width, mask, racc,
        cacc=None, cmask=None, diagonal=False, rows_of=None,
    ):
        if rows_of is None:
            rows_of = right[pl.ds(r0, width), :]
            allowed = mask[0:1, pl.ds(r0, width)]
        else:
            allowed = mask
        similar = dot_t(left[pl.ds(l0, height), :], rows_of)
        total = jnp.zeros((8, width), f32)
        for c in range(height // 32):
            block = similar[c * 32 : (c + 1) * 32, :]
            w = 1.0 / (1.0 + jnp.exp2(block * SCALE + SHIFT))
            if diagonal:
                here = l0 + c * 32 + lax.broadcasted_iota(jnp.int32, (32, width), 0)
                there = r0 + lax.broadcasted_iota(jnp.int32, (32, width), 1)
                w = jnp.where(here == there, 0.0, w)
            rows = pl.ds(l0 + c * 32, 32)
            wr = w * allowed
            if width == 256:
                wr = wr[:, :128] + wr[:, 128:]
            racc[rows, :] += wr
            if cacc is not None:
                cm = cmask[rows, :]
                if width == 256:
                    cm = jnp.concatenate([cm, cm], axis=1)
                wc = w * cm
                total = total + wc[0:8] + wc[8:16] + wc[16:24] + wc[24:32]
        if right is None:
            cacc[0, :, pl.ds(r0, PART)] += total[:, :PART]
            cacc[1, :, pl.ds(r0, PART)] += total[:, PART:]
        elif cacc is not None:
            cacc[:, pl.ds(r0, width)] += total

    def fill_lane(mask, block, r0, size):
        rows = pl.ds(r0, size)
        mask[:, rows] = lane_mask(block[rows, :128])

    def fill_row(mask, block, r0, size):
        rows = pl.ds(r0, size)
        mask[rows, :] = row_mask(block[rows, :128])

    def own_own(l, h):
        meet(own, l * 256, 256, own, h * 256, 256, m_own, r_own, diagonal=l == h)

    def own_p0(l, h):
        meet(own, l * 256, 256, p0, h * 256, 256, m_p0, r_own)

    def own_near(j, r0, width):
        for l0 in (0, 256):
            meet(
                own, l0, 256, near.at[j], r0, width, m_near.at[j], r_own,
                c_near.at[j], mc_own,
            )

    def own_both(r0):
        cols = pl.ds(r0, PART)
        rows_of = jnp.concatenate([near[0, cols, :], near[1, cols, :]], axis=0)
        allowed = jnp.concatenate([m_near[0, 0:1, cols], m_near[1, 0:1, cols]], axis=1)
        for l0 in (0, 256):
            meet(
                own, l0, 256, None, r0, 256, allowed, r_own,
                c_near, mc_own, rows_of=rows_of,
            )

    def back_near(l0, height, r0, width):
        meet(
            back, l0, height, near.at[pick], r0, width, m_near.at[pick], r_back,
            c_near.at[pick], mc_back,
        )

    def landed(g):
        for r in range(4 * g, 4 * g + 4):
            to_near[r].wait_recv()
        to_mate[g].start()
        fill_lane(m_near.at[0], near.at[0], g * PART, PART)

    def behind(g):
        for r in range(4 * g, 4 * g + 4):
            to_back[r].wait_recv()
        fill_row(mc_back, back, g * PART, PART)

    def mated(g):
        to_mate[g].wait_recv()
        fill_lane(m_near.at[1], near.at[1], g * PART, PART)

    for n in range(16):
        if n:
            exchange(n).wait_recv()
        if n + AHEAD + 1 < 16:
            exchange(n + AHEAD + 1).start()
        to_near[n].start()
        to_back[n].start()
        if n % 8 == 7:
            to_p0[n // 8].start()
        if n == 8:
            fill_lane(m_own, own, 0, 256)
            fill_row(mc_own, own, 0, 256)
        if n == 9:
            own_own(0, 0)
        if n == 10:
            landed(0)
        if n == 11:
            to_p0[0].wait_recv()
            fill_lane(m_p0, p0, 0, 256)
        if n == 12:
            own_p0(0, 0)
    fill_lane(m_own, own, 256, 256)
    fill_row(mc_own, own, 256, 256)
    landed(1)
    own_own(0, 1)
    own_own(1, 0)
    own_own(1, 1)
    own_near(0, 0, 256)
    mated(0)
    mated(1)
    own_near(1, 0, 256)
    behind(0)
    behind(1)
    back_near(0, 256, 0, 256)
    to_p0[1].wait_recv()
    fill_lane(m_p0, p0, 256, 256)
    landed(2)
    behind(2)
    back_near(256, PART, 0, 256)
    mated(2)
    own_both(256)
    back_near(0, 256, 256, PART)
    back_near(256, PART, 256, PART)
    landed(3)
    behind(3)
    back_near(384, PART, 0, 256)
    back_near(384, PART, 256, PART)
    mated(3)
    back_near(0, 256, 384, PART)
    back_near(256, 256, 384, PART)

    def give_back(j, device):
        return pltpu.make_async_remote_copy(
            src_ref=ret_out.at[j],
            dst_ref=ret_in.at[j],
            send_sem=rs.at[j],
            recv_sem=rr.at[j],
            device_id=device,
            device_id_type=MESH,
        )

    backs = [give_back(0, up), give_back(1, up_mate), give_back(2, down)]

    def turned(racc):
        left = racc[...]
        done = jnp.zeros((8, BLOCK), f32)
        for _ in range(3):
            part = left.astype(bf16)
            left = left - part.astype(f32)
            done = done + dot_t(sum_row, part)
        return done

    ret_out[2] = turned(r_back)[0:1]
    backs[2].start()
    own_both(384)
    ret_out[0] = jnp.sum(c_near[0], axis=0, keepdims=True)
    backs[0].start()
    ret_out[1] = jnp.sum(c_near[1], axis=0, keepdims=True)
    backs[1].start()
    own_p0(1, 0)
    own_p0(0, 1)
    own_p0(1, 1)
    total = turned(r_own)[0:1]
    for sent in backs:
        sent.wait_recv()
    for j in range(3):
        total = total + ret_in[j]
    for j in range(4):
        fin_out[j] = total[:, j * PART : (j + 1) * PART]
    fin_in[0] = fin_out[0]

    def finish(r):
        dx, dy = TURNS[r]
        return pltpu.make_async_remote_copy(
            src_ref=fin_out.at[r // 4],
            dst_ref=fin_in.at[r],
            send_sem=fs.at[r],
            recv_sem=fr.at[r],
            device_id=plane(4 - dx, 4 - dy),
            device_id_type=MESH,
        )

    for r in range(15, 0, -1):
        finish(r).start()
    wanted = (slots == rank).astype(f32)
    chosen = jnp.concatenate(
        [(cluster == cluster_of(r)).astype(f32) for r in range(16)], axis=0
    )
    for r in range(1, 16):
        finish(r).wait_recv()
    sums = jnp.concatenate(
        [fin_in[r][:, (r % 4) * SLOT : (r % 4 + 1) * SLOT] for r in range(16)], axis=0
    )
    found = jnp.dot(sums, wanted, preferred_element_type=f32, precision=lax.Precision.HIGHEST)
    result[...] = jnp.sum(found * chosen, axis=0, keepdims=True)

    for r in range(16):
        if r:
            exchange(r).wait_send()
            finish(r).wait_send()
        to_near[r].wait_send()
        to_back[r].wait_send()
    for h in range(2):
        to_p0[h].wait_send()
    for g in range(4):
        to_mate[g].wait_send()
    for sent in backs:
        sent.wait_send()


def shards(embeddings, cluster_ids):
    dma = pltpu.SemaphoreType.DMA
    block = pltpu.VMEM((BLOCK, FEAT), bf16)
    racc = pltpu.VMEM((BLOCK, 128), f32)
    cacc = pltpu.VMEM((8, BLOCK), f32)
    soft = pl.pallas_call(
        kernel,
        out_shape=jax.ShapeDtypeStruct((1, ROWS), f32),
        in_specs=[pl.BlockSpec(memory_space=pltpu.HBM)] * 2,
        out_specs=pl.BlockSpec(memory_space=pltpu.VMEM),
        scratch_shapes=[
            pltpu.VMEM((ROWS, FEAT), bf16),
            pltpu.VMEM((1, ROWS), jnp.int32),
            pltpu.VMEM((ROWS, FEAT), bf16),
            block, block,
            pltpu.VMEM((2, BLOCK, FEAT), bf16),
            block, block,
            racc, racc,
            pltpu.VMEM((2, 8, BLOCK), f32),
            cacc, cacc,
            pltpu.VMEM((2, 8, BLOCK), f32),
            racc, racc,
            pltpu.VMEM((3, 1, BLOCK), f32),
            pltpu.VMEM((3, 1, BLOCK), f32),
            pltpu.VMEM((4, 1, PART), f32),
            pltpu.VMEM((16, 1, PART), f32),
            dma((5,)),
            dma((16,)), dma((16,)),
            dma((16,)), dma((16,)), dma((16,)), dma((16,)),
            dma((2,)), dma((2,)), dma((4,)), dma((4,)),
            dma((3,)), dma((3,)),
            dma((16,)), dma((16,)),
        ],
        compiler_params=pltpu.CompilerParams(
            collective_id=0, has_side_effects=True, vmem_limit_bytes=LIMIT
        ),
    )(embeddings, cluster_ids.reshape(1, ROWS))
    return jnp.log1p(soft.reshape(ROWS))


def solution(mesh):
    return jax.shard_map(
        shards,
        mesh=mesh,
        in_specs=(P(("grp", "blk"), None), P(("grp", "blk"))),
        out_specs=P(("grp", "blk")),
        check_vma=False,
    )
```

```python
import functools

import jax
import jax.numpy as jnp
from jax import lax
from jax.experimental import pallas as pl
from jax.experimental.pallas import tpu as pltpu
from jax.sharding import PartitionSpec as P

MESH = pl.DeviceIdType.MESH
ROWS = 256
FEAT = 1024
SLOT = 32
BLOCK = 16 * SLOT
PART = 4 * SLOT
TURNS = (
    (0, 0), (0, 1), (1, 0), (0, 3), (3, 0), (1, 1), (3, 3), (1, 3),
    (3, 1), (0, 2), (2, 0), (2, 1), (1, 2), (2, 3), (3, 2), (2, 2),
)
AHEAD = 8
LIMIT = 67043328
LOG2E = 1.4426950408889634
SCALE = -20.0 * LOG2E
SHIFT = 14.0 * LOG2E
MARK = 1.5
f32 = jnp.float32
bf16 = jnp.bfloat16


def dot_t(a, b, precision=None):
    return lax.dot_general(
        a, b, (((1,), (1,)), ((), ())), preferred_element_type=f32, precision=precision
    )


def kernel(
    emb_hbm, ids_hbm, result,
    emb, ids, unit, out, own, near, back, p0,
    r_own, r_back, c_near, m_own, m_p0, m_near, mc_own, mc_back,
    ret_out, ret_in, fin_out, fin_in,
    es, p1s, p1r, ns, nr, bs, br, p0s, p0r, xs, xr, rs, rr, fs, fr,
):
    z = lax.axis_index("grp")
    b = lax.axis_index("blk")
    x = b // 8
    y = lax.rem(b // 2, 4)
    k = lax.rem(b, 2)

    def at(xx, yy, zz, kk):
        return (zz, xx * 8 + yy * 2 + kk)

    z_up = lax.rem(z + 1, 4)
    z_down = lax.rem(z + 3, 4)
    up = at(x, y, z_up, k)
    down = at(x, y, z_down, k)
    up_mate = at(x, y, z_up, 1 - k)
    down_mate = at(x, y, z_down, 1 - k)
    mate = at(x, y, z, 1 - k)
    pick = z // 2

    def plane(dx, dy):
        return at(lax.rem(x + dx, 4), lax.rem(y + dy, 4), z, k)

    def piece(r, count=1):
        return pl.ds(r * SLOT, count * SLOT)

    barrier = pltpu.get_barrier_semaphore()
    peers = [plane(r // 4, r % 4) for r in range(1, 16)] + [
        up, down, mate, up_mate, down_mate
    ]
    fetches = [
        pltpu.make_async_copy(
            emb_hbm.at[pl.ds(c * 64, 64), :], emb.at[pl.ds(c * 64, 64), :], es.at[c]
        )
        for c in range(4)
    ]
    fetch_ids = pltpu.make_async_copy(ids_hbm, ids, es.at[4])
    fetch_ids.start()
    for fetch in fetches:
        fetch.start()
    for peer in peers:
        pl.semaphore_signal(barrier, inc=1, device_id=peer, device_id_type=MESH)

    for c in range(4):
        rows = pl.ds(c * 64, 64)
        fetches[c].wait()
        wide = emb[rows, :].astype(f32)
        squared = jnp.sum(wide * wide, axis=1, keepdims=True) + 1e-06
        unit[rows, :] = (wide * lax.rsqrt(squared)).astype(bf16)
    fetch_ids.wait()
    cluster = ids[...]
    hot = (cluster == lax.broadcasted_iota(jnp.int32, (16, ROWS), 0)).astype(f32)
    before = (
        lax.broadcasted_iota(jnp.int32, (ROWS, ROWS), 0)
        < lax.broadcasted_iota(jnp.int32, (ROWS, ROWS), 1)
    ).astype(f32).astype(bf16)
    ranks = jnp.dot(hot.astype(bf16), before, preferred_element_type=f32)
    rank = jnp.sum(hot * ranks, axis=0, keepdims=True).astype(jnp.int32)
    position = cluster * SLOT + rank
    first_lane = lax.broadcasted_iota(jnp.int32, (PART, 128), 1) == 0

    def exchange(r):
        return pltpu.make_async_remote_copy(
            src_ref=out.at[piece(r), :],
            dst_ref=own.at[piece(r), :],
            send_sem=p1s.at[r],
            recv_sem=p1r.at[r],
            device_id=plane(*TURNS[r]),
            device_id_type=MESH,
        )

    def cluster_of(r):
        dx, dy = TURNS[r]
        return lax.rem(x + dx, 4) * 4 + lax.rem(y + dy, 4)

    slots = lax.broadcasted_iota(jnp.int32, (SLOT, ROWS), 0)
    for g in range(4):
        placed = jnp.concatenate(
            [
                (slots + cluster_of(r) * SLOT == position).astype(f32)
                for r in range(4 * g, 4 * g + 4)
            ],
            axis=0,
        )
        empty = jnp.sum(placed, axis=1, keepdims=True) < 0.5
        placed = placed.astype(bf16)
        for c in range(4):
            cols = pl.ds(c * 256, 256)
            moved = jnp.dot(placed, unit[:, cols], preferred_element_type=f32)
            if c == 0:
                head = jnp.where(first_lane & empty, MARK, moved[:, :128])
                moved = jnp.concatenate([head, moved[:, 128:]], axis=1)
            moved = moved.astype(bf16)
            if g == 0:
                own[piece(0), cols] = moved[:SLOT, :]
            out[piece(4 * g, 4), cols] = moved

    pl.semaphore_wait(barrier, len(peers))
    for r in range(1, 1 + AHEAD):
        exchange(r).start()

    for sums in (r_own, r_back, c_near):
        sums[...] = jnp.zeros_like(sums)

    def pass_on(r, src, dst, send, recv, device):
        return pltpu.make_async_remote_copy(
            src_ref=src.at[piece(r), :],
            dst_ref=dst.at[piece(r), :],
            send_sem=send.at[r],
            recv_sem=recv.at[r],
            device_id=device,
            device_id_type=MESH,
        )

    def share(n, size, src, dst, send, recv):
        rows = pl.ds(n * size, size)
        return pltpu.make_async_remote_copy(
            src_ref=src.at[rows, :],
            dst_ref=dst.at[rows, :],
            send_sem=send.at[n],
            recv_sem=recv.at[n],
            device_id=mate,
            device_id_type=MESH,
        )

    to_near = [pass_on(r, own, near.at[0], ns, nr, down) for r in range(16)]
    to_back = [pass_on(r, own, back, bs, br, up) for r in range(16)]
    to_p0 = [share(h, 256, own, p0, p0s, p0r) for h in range(2)]
    to_mate = [share(g, PART, near.at[0], near.at[1], xs, xr) for g in range(4)]

    pick_row = (lax.broadcasted_iota(jnp.int32, (8, 128), 1) == 0).astype(f32).astype(bf16)
    pick_col = (lax.broadcasted_iota(jnp.int32, (128, 128), 0) == 0).astype(f32).astype(bf16)
    sum_row = (lax.broadcasted_iota(jnp.int32, (8, 128), 0) == 0).astype(f32).astype(bf16)

    def lane_mask(block):
        return jnp.where(dot_t(pick_row, block[:, :128]) > 1.25, 0.0, 1.0)

    def row_mask(block):
        marks = jnp.dot(block[:, :128], pick_col, preferred_element_type=f32)
        return jnp.where(marks > 1.25, 0.0, 1.0)

    def meet(
        left, l0, height, right, r0, width, mask, racc,
        cacc=None, cmask=None, diagonal=False, rows_of=None,
    ):
        if rows_of is None:
            rows_of = right[pl.ds(r0, width), :]
            allowed = mask[0:1, pl.ds(r0, width)]
        else:
            allowed = mask
        similar = dot_t(left[pl.ds(l0, height), :], rows_of)
        total = jnp.zeros((8, width), f32)
        for c in range(height // 32):
            block = similar[c * 32 : (c + 1) * 32, :]
            w = 1.0 / (1.0 + jnp.exp2(block * SCALE + SHIFT))
            if diagonal:
                here = l0 + c * 32 + lax.broadcasted_iota(jnp.int32, (32, width), 0)
                there = r0 + lax.broadcasted_iota(jnp.int32, (32, width), 1)
                w = jnp.where(here == there, 0.0, w)
            rows = pl.ds(l0 + c * 32, 32)
            wr = w * allowed
            if width == 256:
                wr = wr[:, :128] + wr[:, 128:]
            racc[rows, :] += wr
            if cacc is not None:
                cm = cmask[rows, :]
                if width == 256:
                    cm = jnp.concatenate([cm, cm], axis=1)
                wc = w * cm
                total = total + wc[0:8] + wc[8:16] + wc[16:24] + wc[24:32]
        if right is None:
            cacc[0, :, pl.ds(r0, PART)] += total[:, :PART]
            cacc[1, :, pl.ds(r0, PART)] += total[:, PART:]
        elif cacc is not None:
            cacc[:, pl.ds(r0, width)] += total

    def fill_lane(mask, block, r0, size):
        rows = pl.ds(r0, size)
        mask[:, rows] = lane_mask(block[rows, :128])

    def fill_row(mask, block, r0, size):
        rows = pl.ds(r0, size)
        mask[rows, :] = row_mask(block[rows, :128])

    def own_own(l, h):
        meet(own, l * 256, 256, own, h * 256, 256, m_own, r_own, diagonal=l == h)

    def own_p0(l, h):
        meet(own, l * 256, 256, p0, h * 256, 256, m_p0, r_own)

    def own_near(j, r0, width):
        for l0 in (0, 256):
            meet(
                own, l0, 256, near.at[j], r0, width, m_near.at[j], r_own,
                c_near.at[j], mc_own,
            )

    def own_both(r0):
        cols = pl.ds(r0, PART)
        rows_of = jnp.concatenate([near[0, cols, :], near[1, cols, :]], axis=0)
        allowed = jnp.concatenate([m_near[0, 0:1, cols], m_near[1, 0:1, cols]], axis=1)
        for l0 in (0, 256):
            meet(
                own, l0, 256, None, r0, 256, allowed, r_own,
                c_near, mc_own, rows_of=rows_of,
            )

    def back_near(l0, height, r0, width):
        meet(
            back, l0, height, near.at[pick], r0, width, m_near.at[pick], r_back,
            c_near.at[pick], mc_back,
        )

    def landed(g):
        for r in range(4 * g, 4 * g + 4):
            to_near[r].wait_recv()
        to_mate[g].start()
        fill_lane(m_near.at[0], near.at[0], g * PART, PART)

    def behind(g):
        for r in range(4 * g, 4 * g + 4):
            to_back[r].wait_recv()
        fill_row(mc_back, back, g * PART, PART)

    def mated(g):
        to_mate[g].wait_recv()
        fill_lane(m_near.at[1], near.at[1], g * PART, PART)

    for n in range(16):
        if n:
            exchange(n).wait_recv()
        if n + AHEAD + 1 < 16:
            exchange(n + AHEAD + 1).start()
        to_near[n].start()
        to_back[n].start()
        if n % 8 == 7:
            to_p0[n // 8].start()
        if n == 8:
            fill_lane(m_own, own, 0, 256)
            fill_row(mc_own, own, 0, 256)
        if n == 9:
            own_own(0, 0)
        if n == 10:
            landed(0)
        if n == 11:
            to_p0[0].wait_recv()
            fill_lane(m_p0, p0, 0, 256)
        if n == 12:
            own_p0(0, 0)
    fill_lane(m_own, own, 256, 256)
    fill_row(mc_own, own, 256, 256)
    landed(1)
    own_own(0, 1)
    own_own(1, 0)
    own_own(1, 1)
    own_near(0, 0, 256)
    mated(0)
    mated(1)
    own_near(1, 0, 256)
    behind(0)
    behind(1)
    back_near(0, 256, 0, 256)
    to_p0[1].wait_recv()
    fill_lane(m_p0, p0, 256, 256)
    landed(2)
    behind(2)
    back_near(256, PART, 0, 256)
    mated(2)
    own_both(256)
    back_near(0, 256, 256, PART)
    back_near(256, PART, 256, PART)
    landed(3)
    behind(3)
    back_near(384, PART, 0, 256)
    back_near(384, PART, 256, PART)
    mated(3)
    back_near(0, 256, 384, PART)
    back_near(256, 256, 384, PART)

    def give_back(j, device):
        return pltpu.make_async_remote_copy(
            src_ref=ret_out.at[j],
            dst_ref=ret_in.at[j],
            send_sem=rs.at[j],
            recv_sem=rr.at[j],
            device_id=device,
            device_id_type=MESH,
        )

    backs = [give_back(0, up), give_back(1, up_mate), give_back(2, down)]

    def turned(racc):
        left = racc[...]
        done = jnp.zeros((8, BLOCK), f32)
        for _ in range(3):
            part = left.astype(bf16)
            left = left - part.astype(f32)
            done = done + dot_t(sum_row, part)
        return done

    ret_out[2] = turned(r_back)[0:1]
    backs[2].start()
    own_both(384)
    ret_out[0] = jnp.sum(c_near[0], axis=0, keepdims=True)
    backs[0].start()
    ret_out[1] = jnp.sum(c_near[1], axis=0, keepdims=True)
    backs[1].start()
    own_p0(1, 0)
    own_p0(0, 1)
    own_p0(1, 1)
    total = turned(r_own)[0:1]
    for sent in backs:
        sent.wait_recv()
    for j in range(3):
        total = total + ret_in[j]
    for j in range(4):
        fin_out[j] = total[:, j * PART : (j + 1) * PART]
    fin_in[0] = fin_out[0]

    def finish(r):
        dx, dy = TURNS[r]
        return pltpu.make_async_remote_copy(
            src_ref=fin_out.at[r // 4],
            dst_ref=fin_in.at[r],
            send_sem=fs.at[r],
            recv_sem=fr.at[r],
            device_id=plane(4 - dx, 4 - dy),
            device_id_type=MESH,
        )

    for r in range(15, 0, -1):
        finish(r).start()
    wanted = (slots == rank).astype(f32).astype(bf16)
    chosen = jnp.concatenate(
        [(cluster == cluster_of(r)).astype(f32) for r in range(16)], axis=0
    )
    for r in range(1, 16):
        finish(r).wait_recv()
    sums = jnp.concatenate(
        [fin_in[r][:, (r % 4) * SLOT : (r % 4 + 1) * SLOT] for r in range(16)], axis=0
    )
    found = jnp.zeros((16, ROWS), f32)
    for _ in range(3):
        term = sums.astype(bf16)
        sums = sums - term.astype(f32)
        found = found + jnp.dot(term, wanted, preferred_element_type=f32)
    result[...] = jnp.sum(found * chosen, axis=0, keepdims=True)

    for r in range(16):
        if r:
            exchange(r).wait_send()
            finish(r).wait_send()
        to_near[r].wait_send()
        to_back[r].wait_send()
    for h in range(2):
        to_p0[h].wait_send()
    for g in range(4):
        to_mate[g].wait_send()
    for sent in backs:
        sent.wait_send()


def shards(embeddings, cluster_ids):
    dma = pltpu.SemaphoreType.DMA
    block = pltpu.VMEM((BLOCK, FEAT), bf16)
    racc = pltpu.VMEM((BLOCK, 128), f32)
    cacc = pltpu.VMEM((8, BLOCK), f32)
    soft = pl.pallas_call(
        kernel,
        out_shape=jax.ShapeDtypeStruct((1, ROWS), f32),
        in_specs=[pl.BlockSpec(memory_space=pltpu.HBM)] * 2,
        out_specs=pl.BlockSpec(memory_space=pltpu.VMEM),
        scratch_shapes=[
            pltpu.VMEM((ROWS, FEAT), bf16),
            pltpu.VMEM((1, ROWS), jnp.int32),
            pltpu.VMEM((ROWS, FEAT), bf16),
            block, block,
            pltpu.VMEM((2, BLOCK, FEAT), bf16),
            block, block,
            racc, racc,
            pltpu.VMEM((2, 8, BLOCK), f32),
            cacc, cacc,
            pltpu.VMEM((2, 8, BLOCK), f32),
            racc, racc,
            pltpu.VMEM((3, 1, BLOCK), f32),
            pltpu.VMEM((3, 1, BLOCK), f32),
            pltpu.VMEM((4, 1, PART), f32),
            pltpu.VMEM((16, 1, PART), f32),
            dma((5,)),
            dma((16,)), dma((16,)),
            dma((16,)), dma((16,)), dma((16,)), dma((16,)),
            dma((2,)), dma((2,)), dma((4,)), dma((4,)),
            dma((3,)), dma((3,)),
            dma((16,)), dma((16,)),
        ],
        compiler_params=pltpu.CompilerParams(
            collective_id=0, has_side_effects=True, vmem_limit_bytes=LIMIT
        ),
    )(embeddings, cluster_ids.reshape(1, ROWS))
    return jnp.log1p(soft.reshape(ROWS))


def solution(mesh):
    return jax.shard_map(
        shards,
        mesh=mesh,
        in_specs=(P(("grp", "blk"), None), P(("grp", "blk"))),
        out_specs=P(("grp", "blk")),
        check_vma=False,
    )
```

```python
import functools

import jax
import jax.numpy as jnp
from jax import lax
from jax.experimental import pallas as pl
from jax.experimental.pallas import tpu as pltpu
from jax.sharding import PartitionSpec as P

MESH = pl.DeviceIdType.MESH
ROWS = 256
FEAT = 1024
SLOT = 32
BLOCK = 16 * SLOT
PART = 4 * SLOT
TURNS = (
    (0, 0), (0, 1), (1, 0), (0, 3), (3, 0), (1, 1), (3, 3), (1, 3),
    (3, 1), (0, 2), (2, 0), (2, 1), (1, 2), (2, 3), (3, 2), (2, 2),
)
AHEAD = 8
LIMIT = 67043328
LOG2E = 1.4426950408889634
SCALE = -20.0 * LOG2E
SHIFT = 14.0 * LOG2E
MARK = 1.5
f32 = jnp.float32
bf16 = jnp.bfloat16


def dot_t(a, b, precision=None):
    return lax.dot_general(
        a, b, (((1,), (1,)), ((), ())), preferred_element_type=f32, precision=precision
    )


def kernel(
    emb_hbm, ids_hbm, result,
    emb, ids, unit, out, own, near, back, p0,
    r_own, r_back, c_near, m_own, m_p0, m_near, mc_own, mc_back,
    ret_out, ret_in, fin_out, fin_in,
    es, p1s, p1r, ns, nr, bs, br, p0s, p0r, xs, xr, rs, rr, fs, fr,
):
    z = lax.axis_index("grp")
    b = lax.axis_index("blk")
    x = b // 8
    y = lax.rem(b // 2, 4)
    k = lax.rem(b, 2)

    def at(xx, yy, zz, kk):
        return (zz, xx * 8 + yy * 2 + kk)

    z_up = lax.rem(z + 1, 4)
    z_down = lax.rem(z + 3, 4)
    up = at(x, y, z_up, k)
    down = at(x, y, z_down, k)
    up_mate = at(x, y, z_up, 1 - k)
    down_mate = at(x, y, z_down, 1 - k)
    mate = at(x, y, z, 1 - k)
    pick = z // 2

    def plane(dx, dy):
        return at(lax.rem(x + dx, 4), lax.rem(y + dy, 4), z, k)

    def piece(r, count=1):
        return pl.ds(r * SLOT, count * SLOT)

    barrier = pltpu.get_barrier_semaphore()
    peers = [plane(r // 4, r % 4) for r in range(1, 16)] + [
        up, down, mate, up_mate, down_mate
    ]
    fetches = [
        pltpu.make_async_copy(
            emb_hbm.at[pl.ds(c * 64, 64), :], emb.at[pl.ds(c * 64, 64), :], es.at[c]
        )
        for c in range(4)
    ]
    fetch_ids = pltpu.make_async_copy(ids_hbm, ids, es.at[4])
    fetch_ids.start()
    for fetch in fetches:
        fetch.start()
    for peer in peers:
        pl.semaphore_signal(barrier, inc=1, device_id=peer, device_id_type=MESH)

    for c in range(4):
        rows = pl.ds(c * 64, 64)
        fetches[c].wait()
        wide = emb[rows, :].astype(f32)
        squared = jnp.sum(wide * wide, axis=1, keepdims=True) + 1e-06
        unit[rows, :] = (wide * lax.rsqrt(squared)).astype(bf16)
    fetch_ids.wait()
    cluster = ids[...]
    hot = (cluster == lax.broadcasted_iota(jnp.int32, (16, ROWS), 0)).astype(f32)
    before = (
        lax.broadcasted_iota(jnp.int32, (ROWS, ROWS), 0)
        < lax.broadcasted_iota(jnp.int32, (ROWS, ROWS), 1)
    ).astype(f32).astype(bf16)
    ranks = jnp.dot(hot.astype(bf16), before, preferred_element_type=f32)
    rank = jnp.sum(hot * ranks, axis=0, keepdims=True).astype(jnp.int32)
    position = cluster * SLOT + rank
    first_lane = lax.broadcasted_iota(jnp.int32, (PART, 128), 1) == 0

    def exchange(r):
        return pltpu.make_async_remote_copy(
            src_ref=out.at[piece(r), :],
            dst_ref=own.at[piece(r), :],
            send_sem=p1s.at[r],
            recv_sem=p1r.at[r],
            device_id=plane(*TURNS[r]),
            device_id_type=MESH,
        )

    def cluster_of(r):
        dx, dy = TURNS[r]
        return lax.rem(x + dx, 4) * 4 + lax.rem(y + dy, 4)

    slots = lax.broadcasted_iota(jnp.int32, (SLOT, ROWS), 0)
    for g in range(4):
        placed = jnp.concatenate(
            [
                (slots + cluster_of(r) * SLOT == position).astype(f32)
                for r in range(4 * g, 4 * g + 4)
            ],
            axis=0,
        )
        empty = jnp.sum(placed, axis=1, keepdims=True) < 0.5
        placed = placed.astype(bf16)
        for c in range(4):
            cols = pl.ds(c * 256, 256)
            moved = jnp.dot(placed, unit[:, cols], preferred_element_type=f32)
            if c == 0:
                head = jnp.where(first_lane & empty, MARK, moved[:, :128])
                moved = jnp.concatenate([head, moved[:, 128:]], axis=1)
            moved = moved.astype(bf16)
            if g == 0:
                own[piece(0), cols] = moved[:SLOT, :]
            out[piece(4 * g, 4), cols] = moved

    pl.semaphore_wait(barrier, len(peers))
    for r in range(1, 1 + AHEAD):
        exchange(r).start()

    for sums in (r_own, r_back, c_near):
        sums[...] = jnp.zeros_like(sums)

    def pass_on(r, src, dst, send, recv, device):
        return pltpu.make_async_remote_copy(
            src_ref=src.at[piece(r), :],
            dst_ref=dst.at[piece(r), :],
            send_sem=send.at[r],
            recv_sem=recv.at[r],
            device_id=device,
            device_id_type=MESH,
        )

    def share(n, size, src, dst, send, recv):
        rows = pl.ds(n * size, size)
        return pltpu.make_async_remote_copy(
            src_ref=src.at[rows, :],
            dst_ref=dst.at[rows, :],
            send_sem=send.at[n],
            recv_sem=recv.at[n],
            device_id=mate,
            device_id_type=MESH,
        )

    to_near = [pass_on(r, own, near.at[0], ns, nr, down) for r in range(16)]
    to_back = [pass_on(r, own, back, bs, br, up) for r in range(16)]
    to_p0 = [share(h, 256, own, p0, p0s, p0r) for h in range(2)]
    to_mate = [share(g, PART, near.at[0], near.at[1], xs, xr) for g in range(4)]

    pick_row = (lax.broadcasted_iota(jnp.int32, (8, 128), 1) == 0).astype(f32).astype(bf16)
    pick_col = (lax.broadcasted_iota(jnp.int32, (128, 128), 0) == 0).astype(f32).astype(bf16)
    sum_row = (lax.broadcasted_iota(jnp.int32, (8, 128), 0) == 0).astype(f32).astype(bf16)

    def lane_mask(block):
        return jnp.where(dot_t(pick_row, block[:, :128]) > 1.25, 0.0, 1.0)

    def row_mask(block):
        marks = jnp.dot(block[:, :128], pick_col, preferred_element_type=f32)
        return jnp.where(marks > 1.25, 0.0, 1.0)

    def meet(
        left, l0, height, right, r0, width, mask, racc,
        cacc=None, cmask=None, diagonal=False, rows_of=None,
    ):
        if rows_of is None:
            rows_of = right[pl.ds(r0, width), :]
            allowed = mask[0:1, pl.ds(r0, width)]
        else:
            allowed = mask
        similar = dot_t(left[pl.ds(l0, height), :], rows_of)
        total = jnp.zeros((8, width), f32)
        for c in range(height // 32):
            block = similar[c * 32 : (c + 1) * 32, :]
            w = 1.0 / (1.0 + jnp.exp2(block * SCALE + SHIFT))
            if diagonal:
                here = l0 + c * 32 + lax.broadcasted_iota(jnp.int32, (32, width), 0)
                there = r0 + lax.broadcasted_iota(jnp.int32, (32, width), 1)
                w = jnp.where(here == there, 0.0, w)
            rows = pl.ds(l0 + c * 32, 32)
            wr = w * allowed
            if width == 256:
                wr = wr[:, :128] + wr[:, 128:]
            racc[rows, :] += wr
            if cacc is not None:
                cm = cmask[rows, :]
                if width == 256:
                    cm = jnp.concatenate([cm, cm], axis=1)
                wc = w * cm
                total = total + wc[0:8] + wc[8:16] + wc[16:24] + wc[24:32]
        if right is None:
            cacc[0, :, pl.ds(r0, PART)] += total[:, :PART]
            cacc[1, :, pl.ds(r0, PART)] += total[:, PART:]
        elif cacc is not None:
            cacc[:, pl.ds(r0, width)] += total

    def fill_lane(mask, block, r0, size):
        rows = pl.ds(r0, size)
        mask[:, rows] = lane_mask(block[rows, :128])

    def fill_row(mask, block, r0, size):
        rows = pl.ds(r0, size)
        mask[rows, :] = row_mask(block[rows, :128])

    def own_own(l, h):
        meet(own, l * 256, 256, own, h * 256, 256, m_own, r_own, diagonal=l == h)

    def own_p0(l, h):
        meet(own, l * 256, 256, p0, h * 256, 256, m_p0, r_own)

    def own_near(j, r0, width):
        for l0 in (0, 256):
            meet(
                own, l0, 256, near.at[j], r0, width, m_near.at[j], r_own,
                c_near.at[j], mc_own,
            )

    def own_both(r0):
        cols = pl.ds(r0, PART)
        rows_of = jnp.concatenate([near[0, cols, :], near[1, cols, :]], axis=0)
        allowed = jnp.concatenate([m_near[0, 0:1, cols], m_near[1, 0:1, cols]], axis=1)
        for l0 in (0, 256):
            meet(
                own, l0, 256, None, r0, 256, allowed, r_own,
                c_near, mc_own, rows_of=rows_of,
            )

    def back_near(l0, height, r0, width):
        meet(
            back, l0, height, near.at[pick], r0, width, m_near.at[pick], r_back,
            c_near.at[pick], mc_back,
        )

    def landed(g):
        for r in range(4 * g, 4 * g + 4):
            to_near[r].wait_recv()
        to_mate[g].start()
        fill_lane(m_near.at[0], near.at[0], g * PART, PART)

    def behind(g):
        for r in range(4 * g, 4 * g + 4):
            to_back[r].wait_recv()
        fill_row(mc_back, back, g * PART, PART)

    def mated(g):
        to_mate[g].wait_recv()
        fill_lane(m_near.at[1], near.at[1], g * PART, PART)

    for n in range(16):
        if n:
            exchange(n).wait_recv()
        if n + AHEAD + 1 < 16:
            exchange(n + AHEAD + 1).start()
        to_near[n].start()
        to_back[n].start()
        if n % 8 == 7:
            to_p0[n // 8].start()
        if n == 8:
            fill_lane(m_own, own, 0, 256)
            fill_row(mc_own, own, 0, 256)
        if n == 9:
            own_own(0, 0)
        if n == 10:
            landed(0)
        if n == 11:
            to_p0[0].wait_recv()
            fill_lane(m_p0, p0, 0, 256)
        if n == 12:
            own_p0(0, 0)
    fill_lane(m_own, own, 256, 256)
    fill_row(mc_own, own, 256, 256)
    landed(1)
    own_own(0, 1)
    own_own(1, 0)
    own_own(1, 1)
    own_near(0, 0, 256)
    mated(0)
    mated(1)
    own_near(1, 0, 256)
    behind(0)
    behind(1)
    back_near(0, 256, 0, 256)
    to_p0[1].wait_recv()
    fill_lane(m_p0, p0, 256, 256)
    landed(2)
    behind(2)
    back_near(256, PART, 0, 256)
    mated(2)
    own_both(256)
    back_near(0, 256, 256, PART)
    back_near(256, PART, 256, PART)
    landed(3)
    behind(3)
    back_near(384, PART, 0, 256)
    back_near(384, PART, 256, PART)
    own_p0(1, 0)
    mated(3)
    back_near(0, 256, 384, PART)
    back_near(256, 256, 384, PART)

    def give_back(j, device):
        return pltpu.make_async_remote_copy(
            src_ref=ret_out.at[j],
            dst_ref=ret_in.at[j],
            send_sem=rs.at[j],
            recv_sem=rr.at[j],
            device_id=device,
            device_id_type=MESH,
        )

    backs = [give_back(0, up), give_back(1, up_mate), give_back(2, down)]

    def turned(racc):
        left = racc[...]
        done = jnp.zeros((8, BLOCK), f32)
        for _ in range(3):
            part = left.astype(bf16)
            left = left - part.astype(f32)
            done = done + dot_t(sum_row, part)
        return done

    ret_out[2] = turned(r_back)[0:1]
    backs[2].start()
    own_both(384)
    ret_out[0] = jnp.sum(c_near[0], axis=0, keepdims=True)
    backs[0].start()
    ret_out[1] = jnp.sum(c_near[1], axis=0, keepdims=True)
    backs[1].start()
    own_p0(0, 1)
    own_p0(1, 1)
    total = turned(r_own)[0:1]
    for sent in backs:
        sent.wait_recv()
    for j in range(3):
        total = total + ret_in[j]
    for j in range(4):
        fin_out[j] = total[:, j * PART : (j + 1) * PART]
    fin_in[0] = fin_out[0]

    def finish(r):
        dx, dy = TURNS[r]
        return pltpu.make_async_remote_copy(
            src_ref=fin_out.at[r // 4],
            dst_ref=fin_in.at[r],
            send_sem=fs.at[r],
            recv_sem=fr.at[r],
            device_id=plane(4 - dx, 4 - dy),
            device_id_type=MESH,
        )

    for r in range(15, 0, -1):
        finish(r).start()
    wanted = (slots == rank).astype(f32).astype(bf16)
    chosen = jnp.concatenate(
        [(cluster == cluster_of(r)).astype(f32) for r in range(16)], axis=0
    )
    for r in range(1, 16):
        finish(r).wait_recv()
    sums = jnp.concatenate(
        [fin_in[r][:, (r % 4) * SLOT : (r % 4 + 1) * SLOT] for r in range(16)], axis=0
    )
    found = jnp.zeros((16, ROWS), f32)
    for _ in range(3):
        term = sums.astype(bf16)
        sums = sums - term.astype(f32)
        found = found + jnp.dot(term, wanted, preferred_element_type=f32)
    result[...] = jnp.sum(found * chosen, axis=0, keepdims=True)

    for r in range(16):
        if r:
            exchange(r).wait_send()
            finish(r).wait_send()
        to_near[r].wait_send()
        to_back[r].wait_send()
    for h in range(2):
        to_p0[h].wait_send()
    for g in range(4):
        to_mate[g].wait_send()
    for sent in backs:
        sent.wait_send()


def shards(embeddings, cluster_ids):
    dma = pltpu.SemaphoreType.DMA
    block = pltpu.VMEM((BLOCK, FEAT), bf16)
    racc = pltpu.VMEM((BLOCK, 128), f32)
    cacc = pltpu.VMEM((8, BLOCK), f32)
    soft = pl.pallas_call(
        kernel,
        out_shape=jax.ShapeDtypeStruct((1, ROWS), f32),
        in_specs=[pl.BlockSpec(memory_space=pltpu.HBM)] * 2,
        out_specs=pl.BlockSpec(memory_space=pltpu.VMEM),
        scratch_shapes=[
            pltpu.VMEM((ROWS, FEAT), bf16),
            pltpu.VMEM((1, ROWS), jnp.int32),
            pltpu.VMEM((ROWS, FEAT), bf16),
            block, block,
            pltpu.VMEM((2, BLOCK, FEAT), bf16),
            block, block,
            racc, racc,
            pltpu.VMEM((2, 8, BLOCK), f32),
            cacc, cacc,
            pltpu.VMEM((2, 8, BLOCK), f32),
            racc, racc,
            pltpu.VMEM((3, 1, BLOCK), f32),
            pltpu.VMEM((3, 1, BLOCK), f32),
            pltpu.VMEM((4, 1, PART), f32),
            pltpu.VMEM((16, 1, PART), f32),
            dma((5,)),
            dma((16,)), dma((16,)),
            dma((16,)), dma((16,)), dma((16,)), dma((16,)),
            dma((2,)), dma((2,)), dma((4,)), dma((4,)),
            dma((3,)), dma((3,)),
            dma((16,)), dma((16,)),
        ],
        compiler_params=pltpu.CompilerParams(
            collective_id=0, has_side_effects=True, vmem_limit_bytes=LIMIT
        ),
    )(embeddings, cluster_ids.reshape(1, ROWS))
    return jnp.log1p(soft.reshape(ROWS))


def solution(mesh):
    return jax.shard_map(
        shards,
        mesh=mesh,
        in_specs=(P(("grp", "blk"), None), P(("grp", "blk"))),
        out_specs=P(("grp", "blk")),
        check_vma=False,
    )
```
